256 devices in a mesh: blk: 64 (over y_hi, z, x), layer: 4 (over y_lo, core).
Axes of the slice: x: 4, y: 4 (y_hi: 2, y_lo: 2; y = y_hi * 2 + y_lo), z: 8, core: 2. Of those that a mesh axis runs over, the one named last changes fastest.
Arguments:
- ref_pos: float32 [64, 4, 3, 8192], P('blk', 'layer'), may hold values from -9 to 9
- disk_disp: float32 [64, 4, 3, 8192], P('blk', 'layer'), may hold values from -2 to 2
- disk_vel: float32 [64, 4, 3, 8192], P('blk', 'layer'), may hold values from -6 to 6
- damage: float32 [64, 4, 8192], P('blk', 'layer'), may hold values from 0 to 0.6
- modulus: float32 [64, 4, 8192], P('blk', 'layer'), may hold values from 0.5 to 2
- body_load: float32 [64, 4, 3, 8192], P('blk', 'layer'), may hold values from -6 to 6
- nbr_tiles: int32 [64, 4, 64, 15], P('blk', 'layer'), may hold values from 0 to 959, as said below
- break_flags: int32 [64, 4, 32], P('blk', 'layer'), may hold values from 0 to 1073741823, as said below
- blade_disp: float32 [64, 4, 3, 512], P('blk', 'layer'), may hold values from -2 to 2
- blade_vel: float32 [64, 4, 3, 512], P('blk', 'layer'), may hold values from -6 to 6
- elem_nodes: int32 [64, 4, 8, 128], P('blk', 'layer'), may hold values from 0 to 511
- elem_modulus: float32 [64, 4, 128], P('blk', 'layer'), may hold values from 0.5 to 2
- elem_stiff: float32 [24, 24], replicated, may hold values from -0.2 to 6, as said below
- root_nodes: int32 [64, 4, 64, 8], P('blk', 'layer'), may hold values from 0 to 511
- rim_points: int32 [64, 4, 64, 8], P('blk', 'layer'), may hold values from 0 to 8191
Outputs:
- disk_disp_new: float32 [64, 4, 3, 8192], P('blk', 'layer')
- disk_vel_new: float32 [64, 4, 3, 8192], P('blk', 'layer')
- blade_disp_new: float32 [64, 4, 3, 512], P('blk', 'layer')
- blade_vel_new: float32 [64, 4, 3, 512], P('blk', 'layer')
The draws below stay inside these ranges and needn't reach their ends.
Inputs may be any that keep to these rules, and one draw needn't show every extreme that they name: `nbr_tiles`: entry k of every list names block k, except where slab l + (k mod 3) - 1 lies outside 0 to 3; there it names block k - (k mod 3) + 1 of the own slab. The tile within the block is arbitrary; tiles may repeat. `break_flags`: only bits 0 to 29 are used; a set bit marks a neighbour tile whose bonds are all broken. `elem_stiff`: Symmetric.
All inputs are finite; a program needn't handle non-finite values.
Results may differ from the reference program's by a relative error of at most 0.0003.
Values sent between devices are 32-bit elements; how exact they have to be, the bound alone decides.
No kernel may reach another device: no remote copies, remote signals or barrier semaphores. Data moves between devices by JAX's collectives and lax.ppermute only.
A program may use at most 64 MiB of HBM per device.

```python
import math
import jax
import jax.numpy as jnp
from jax import lax

TILE = 128
SLOTS = 15
TILE_DEV = 64
BNODE_DEV = 512
ELEM_DEV = 128
CAP = 8
SECTORS = 64
SLABS = 4
PTS_DEV = 8192


def draw_nbr_tiles(key, part):
    picked = jax.random.randint(key, (SECTORS, SLABS, TILE_DEV, SLOTS), 0, TILE_DEV, dtype=jnp.int32)
    slot_ids = jnp.arange(SLOTS, dtype=jnp.int32)[None, None, None, :]
    slab_ids = jnp.arange(SLABS, dtype=jnp.int32)[None, :, None, None]
    slab_step = slot_ids % 3 - 1
    outside = (slab_ids + slab_step < 0) | (slab_ids + slab_step > SLABS - 1)
    block = jnp.where(outside, slot_ids - slab_step, slot_ids)
    return (block * TILE_DEV + picked).astype(jnp.int32)


def draw_break_flags(key, part):
    key_centre = jax.random.fold_in(key, 11)
    key_bits = jax.random.fold_in(key, 12)
    centre = jax.random.randint(key_centre, (), 0, SECTORS, dtype=jnp.int32)
    sector_ids = jnp.arange(SECTORS, dtype=jnp.int32)
    distance = jnp.abs(sector_ids - centre)
    distance = jnp.minimum(distance, SECTORS - distance)
    cracked = distance <= SECTORS // 16
    chance = jnp.where(cracked, 500, 60)[:, None, None, None]
    rolls = jax.random.randint(key_bits, (SECTORS, SLABS, TILE_DEV // 2, 30), 0, 1000, dtype=jnp.int32)
    bits = (rolls < chance).astype(jnp.int32)
    powers = jnp.left_shift(jnp.ones((30,), jnp.int32), jnp.arange(30, dtype=jnp.int32))
    return jnp.sum(bits * powers[None, None, None, :], axis=3).astype(jnp.int32)


def draw_elem_stiff(key, part):
    key_off = jax.random.fold_in(key, 21)
    key_diag = jax.random.fold_in(key, 22)
    base = jax.random.uniform(key_off, (24, 24), jnp.float32, -0.2, 0.2)
    symmetric = (base + base.T) * 0.5
    diag_part = 5.0 + jax.random.uniform(key_diag, (24,), jnp.float32, 0.0, 1.0)
    eye = jnp.eye(24, dtype=jnp.float32)
    return (symmetric * (1.0 - eye) + eye * diag_part[None, :]).astype(jnp.float32)


def set_ends(array, key, smallest, largest):
    longest = array.shape.index(max(array.shape))
    spots = []
    for shift in (0, 1):
        where = [jax.random.randint(jax.random.fold_in(key, axis), (), 0, length) for axis, length in enumerate(array.shape)]
        where[longest] = (where[longest] + shift) % array.shape[longest]
        spots.append(tuple(where))
    return array.at[spots[0]].set(smallest).at[spots[1]].set(largest)


def steps_of(rng, extent, cuts, least, largest):
    def one(dim, parts):
        heights = jax.random.uniform(jax.random.fold_in(jax.random.fold_in(rng, 6), dim), (parts,), jnp.float32, least / len(cuts), largest / len(cuts))
        return jnp.repeat(jnp.exp(heights), extent[dim] // parts).reshape((-1,) + (1,) * (len(extent) - dim - 1))

    loudness = one(*cuts[0])
    for cut in cuts[1:]:
        loudness = loudness * one(*cut)
    return loudness


def normal_values(own_key, dims, scale, reach, shards=(), kind=jnp.bfloat16):
    result = jax.random.normal(own_key, dims, jnp.float32) * scale
    if len(shards) > 0:
        result = steps_of(own_key, dims, shards, -0.22, 0.18) * result
    return jnp.clip(result, min=-reach, max=reach).astype(kind)


def setup_inputs(seed: int = 0) -> dict:
    seeds = jax.random.split(jax.random.key(seed), 16)
    return {
        "ref_pos": normal_values(seeds[0], (SECTORS, SLABS, 3, PTS_DEV), 1.5, 9.0, ((0, 64), (1, 4)), jnp.float32),
        "disk_disp": normal_values(seeds[1], (SECTORS, SLABS, 3, PTS_DEV), 0.3, 2.0, ((0, 64), (1, 4)), jnp.float32),
        "disk_vel": normal_values(seeds[2], (SECTORS, SLABS, 3, PTS_DEV), 1.0, 6.0, ((0, 64), (1, 4)), jnp.float32),
        "damage": jnp.clip(0.6 * jax.random.uniform(seeds[3], (SECTORS, SLABS, PTS_DEV), jnp.float32) ** steps_of(seeds[3], (SECTORS, SLABS, PTS_DEV), ((0, 64), (1, 4)), -0.2, 0.2), 0.0, 0.6),
        "modulus": jnp.clip(jnp.exp(math.log(2.0) - 1.3862944 * jax.random.uniform(seeds[4], (SECTORS, SLABS, PTS_DEV), jnp.float32) ** steps_of(seeds[4], (SECTORS, SLABS, PTS_DEV), ((0, 64), (1, 4)), -0.2, 0.2)), 0.5, 2.0),
        "body_load": normal_values(seeds[5], (SECTORS, SLABS, 3, PTS_DEV), 1.0, 6.0, ((0, 64), (1, 4)), jnp.float32),
        "nbr_tiles": draw_nbr_tiles(jax.random.fold_in(seeds[15], 71), 0),
        "break_flags": draw_break_flags(jax.random.fold_in(seeds[15], 71), 0),
        "blade_disp": normal_values(seeds[8], (SECTORS, SLABS, 3, BNODE_DEV), 0.3, 2.0, ((0, 64), (1, 4)), jnp.float32),
        "blade_vel": normal_values(seeds[9], (SECTORS, SLABS, 3, BNODE_DEV), 1.0, 6.0, ((0, 64), (1, 4)), jnp.float32),
        "elem_nodes": set_ends(jax.random.randint(seeds[10], (SECTORS, SLABS, 8, ELEM_DEV), 0, BNODE_DEV), jax.random.fold_in(seeds[10], 1), 0, BNODE_DEV - 1).astype(jnp.int32),
        "elem_modulus": jnp.clip(jnp.exp(math.log(2.0) - 1.3862944 * jax.random.uniform(seeds[11], (SECTORS, SLABS, ELEM_DEV), jnp.float32) ** steps_of(seeds[11], (SECTORS, SLABS, ELEM_DEV), ((0, 64), (1, 4)), -0.2, 0.2)), 0.5, 2.0),
        "elem_stiff": draw_elem_stiff(jax.random.fold_in(seeds[15], 71), 0),
        "root_nodes": set_ends(jax.random.randint(seeds[13], (SECTORS, SLABS, SECTORS, CAP), 0, BNODE_DEV), jax.random.fold_in(seeds[13], 1), 0, BNODE_DEV - 1).astype(jnp.int32),
        "rim_points": set_ends(jax.random.randint(seeds[14], (SECTORS, SLABS, SECTORS, CAP), 0, PTS_DEV), jax.random.fold_in(seeds[14], 1), 0, PTS_DEV - 1).astype(jnp.int32),
    }


bond_scale = 0.5
spring = 0.5
time_step = 0.5
horizon_sq = 9.0


def pair_force(own_tile, neighbours, alive_row):
    bond_ref = neighbours[:, 0:3, None, :] - own_tile[0:3, :, None]
    bond_now = bond_ref + neighbours[:, 3:6, None, :] - own_tile[3:6, :, None]
    ref_sq = jnp.sum(bond_ref * bond_ref, axis=1)
    now_sq = jnp.sum(bond_now * bond_now, axis=1)
    strain = (now_sq - ref_sq) / (2.0 * (ref_sq + 1.0))
    intact = (1.0 - own_tile[6])[None, :, None] * (1.0 - neighbours[:, 6])[:, None, :]
    stiffness = 0.5 * (own_tile[7][None, :, None] + neighbours[:, 7][:, None, :])
    coeff = bond_scale * stiffness * intact * jnp.exp(-ref_sq / horizon_sq) * strain * alive_row[:, None, None]
    return jnp.sum(coeff[:, None] * bond_now, axis=(0, 3))


def alive_flags(flag_words, tile_count, slot_count):
    tile_ids = jnp.arange(tile_count, dtype=jnp.int32)
    word_tile = flag_words[tile_ids // 2]
    offsets = (tile_ids % 2)[:, None] * slot_count + jnp.arange(slot_count, dtype=jnp.int32)[None, :]
    bits = jnp.right_shift(word_tile[:, None], offsets) & 1
    return (1 - bits).astype(jnp.float32)


def blade_internal(blade_u, connect, elem_scale, stiff):
    elem_count = connect.shape[1]
    gathered = blade_u[:, connect].reshape(24, elem_count)
    elem_force = elem_scale[None, :] * jnp.dot(stiff, gathered, precision=lax.Precision.HIGHEST, preferred_element_type=jnp.float32)
    return jnp.zeros_like(blade_u).at[:, connect.reshape(-1)].add(-elem_force.reshape(3, -1))


def scatter_add(base, index, values):
    return jnp.zeros_like(base).at[:, index].add(values)


def reference(ref_pos, disk_disp, disk_vel, damage, modulus, body_load, nbr_tiles, break_flags, blade_disp, blade_vel, elem_nodes, elem_modulus, elem_stiff, root_nodes, rim_points):
    packed = jnp.concatenate([ref_pos, disk_disp, damage[:, :, None, :], modulus[:, :, None, :]], axis=2)
    tiles = packed.reshape(SECTORS, SLABS, 8, TILE_DEV, TILE).transpose(0, 1, 3, 2, 4)

    def device_force(index):
        sector = index // SLABS
        slab = index % SLABS
        own_tiles = tiles[sector, slab]
        names = nbr_tiles[sector, slab]
        block = names // TILE_DEV
        picked = names % TILE_DEV
        src_sector = (sector + block // 3 - 2) % SECTORS
        src_slab = jnp.clip(slab + block % 3 - 1, 0, SLABS - 1)
        neighbours = tiles[src_sector, src_slab, picked]
        alive_rows = alive_flags(break_flags[sector, slab], TILE_DEV, SLOTS)
        forces = jax.vmap(pair_force)(own_tiles, neighbours, alive_rows)
        return forces.transpose(1, 0, 2).reshape(3, TILE_DEV * TILE)

    bond_force = lax.map(device_force, jnp.arange(SECTORS * SLABS, dtype=jnp.int32)).reshape(SECTORS, SLABS, 3, PTS_DEV)

    rim_flat = rim_points.reshape(SECTORS, SLABS, SECTORS * CAP)
    root_flat = root_nodes.reshape(SECTORS, SLABS, SECTORS * CAP)
    at_rim = jnp.take_along_axis(disk_disp, rim_flat[:, :, None, :], axis=3)
    at_rim = at_rim.reshape(SECTORS, SLABS, 3, SECTORS, CAP).transpose(3, 1, 2, 0, 4).reshape(SECTORS, SLABS, 3, SECTORS * CAP)
    at_root = jnp.take_along_axis(blade_disp, root_flat[:, :, None, :], axis=3)
    loads = spring * (at_rim - at_root)
    coupling = jax.vmap(jax.vmap(scatter_add))(blade_disp, root_flat, loads)
    returned = loads.reshape(SECTORS, SLABS, 3, SECTORS, CAP).transpose(3, 1, 2, 0, 4).reshape(SECTORS, SLABS, 3, SECTORS * CAP)
    reaction = jax.vmap(jax.vmap(scatter_add))(disk_disp, rim_flat, -returned)

    internal = jax.vmap(jax.vmap(blade_internal, in_axes=(0, 0, 0, None)), in_axes=(0, 0, 0, None))(blade_disp, elem_nodes, elem_modulus, elem_stiff)

    disk_vel_new = disk_vel + time_step * (bond_force + body_load + reaction)
    disk_disp_new = disk_disp + time_step * disk_vel_new
    blade_vel_new = blade_vel + time_step * (internal + coupling)
    blade_disp_new = blade_disp + time_step * blade_vel_new
    return (disk_disp_new, disk_vel_new, blade_disp_new, blade_vel_new)
```

```python
import math
import jax
import jax.numpy as jnp
from jax import lax
from jax.experimental import pallas as pl
from jax.experimental.pallas import tpu as pltpu
from jax.sharding import PartitionSpec as P

TILE = 128
log_scale = math.log2(math.e) / 9.0
force_scale = -0.125 * log_scale * math.exp(1.0 / 9.0)
f32 = jnp.float32
bf16 = jnp.bfloat16
UNROLL = 8
OWN_UNROLL = 1
spring = 0.5
time_step = 0.5


def split3(value):
    high = value.astype(bf16).astype(f32)
    rest = value - high
    middle = rest.astype(bf16).astype(f32)
    return high, middle, (rest - middle)


def point_terms(v):
    row = lax.broadcasted_iota(jnp.int32, v.shape, 0)
    disp = pltpu.roll(v, 5, 0)
    now = v + disp
    first = row < 3
    ref_norm = jnp.sum(jnp.where(first, v * v, 0.0), axis=0, keepdims=True)
    growth = jnp.sum(jnp.where(first, disp * (v + now), 0.0), axis=0, keepdims=True)
    return row, disp, now, ref_norm, growth


def own_kernel(field_ref, lhs_ref):
    def one_tile(tile, carry):
        v = field_ref[:, pl.ds(pl.multiple_of(tile * TILE, TILE), TILE)]
        row, disp, now, ref_norm, growth = point_terms(v)
        row16 = lax.broadcasted_iota(jnp.int32, (16, TILE), 0)
        coef_ref = jnp.where(row < 3, 2.0 * log_scale * v, jnp.where(row == 6, -log_scale, 0.0))
        coef_now = jnp.where(
            row < 3,
            -2.0 * disp,
            jnp.where(row < 6, -2.0 * pltpu.roll(now, 3, 0), jnp.where(row == 7, 1.0, 0.0)),
        )
        for place, coef, alone in (
            (0, coef_ref, -log_scale * (1.0 + ref_norm)),
            (1, coef_now, growth),
        ):
            high, middle, low = split3(coef)
            a, b, c = split3(alone)
            const = jnp.where(row16 == 0, a, jnp.where(row16 == 1, b, jnp.where(row16 == 2, c, 0.0)))
            rows = jnp.concatenate([high, high, middle, middle, high, low, const], axis=0)
            lhs_ref[tile, pl.ds(place * TILE, TILE), :] = rows.T.astype(bf16)
        return carry

    lax.fori_loop(0, field_ref.shape[1] // TILE, one_tile, 0, unroll=OWN_UNROLL)


def own_table(field):
    tiles = field.shape[1] // TILE
    return pl.pallas_call(
        own_kernel,
        out_shape=jax.ShapeDtypeStruct((tiles, 2 * TILE, 64), bf16),
        name="own_table",
        cost_estimate=pl.CostEstimate(flops=8_000_000_000, transcendentals=0, bytes_accessed=4_500_000),
    )(field)


def fill_table(field_ref, table_ref, place, chunk):
    def one(step, carry):
        lanes = pl.ds(pl.multiple_of(step * chunk, chunk), chunk)
        v = field_ref[:, lanes]
        row, disp, now, ref_norm, growth = point_terms(v)
        terms = jnp.where(row < 6, v, jnp.where(row == 6, ref_norm, growth))
        high, middle, low = split3(terms)
        table_ref[place, 0:16, lanes] = jnp.concatenate([high, middle], axis=0).astype(bf16)
        table_ref[place, 16:32, lanes] = jnp.concatenate([low, high], axis=0).astype(bf16)
        whole = 1.0 - v[6:7]
        stiff = v[7:8]
        spread = jnp.where(row < 3, now, jnp.where(row < 6, pltpu.roll(now, 3, 0), 1.0))
        weight = whole * jnp.where((row < 3) | (row == 6), 1.0, stiff)
        sums = spread * weight
        q_high = sums.astype(bf16).astype(f32)
        table_ref[place, 32:48, lanes] = jnp.concatenate([q_high, sums - q_high], axis=0).astype(bf16)
        return carry

    lax.fori_loop(0, field_ref.shape[1] // chunk, one, 0)


def make_stage_kernel(slots, first):
    count = len(slots)
    group = 2 if count % 2 == 0 else 3

    def kernel(names_ref, flags_ref, lhs_ref, *refs):
        block_refs = refs[:count]
        rest = refs[count:]
        if not first:
            before_ref, rest = rest[0], rest[1:]
        out_ref, table_ref = rest
        for place, ref in enumerate(block_refs):
            fill_table(ref, table_ref, place, 512)
        ones = jnp.ones((16, TILE), bf16)

        def one_tile(tile, carry):
            lhs = lhs_ref[tile]
            word = flags_ref[tile // 2]
            acc = None
            for start in range(0, count, group):
                rhs, sums = [], []
                for place in range(start, min(start + group, count)):
                    slot = slots[place]
                    name = names_ref[tile, slot]
                    where = (place // 3) * 3 + (name // 64) % 3
                    lanes = pl.ds(pl.multiple_of((name % 64) * TILE, TILE), TILE)
                    top = table_ref[where, 0:16, lanes]
                    low = table_ref[where, 16:32, lanes]
                    alive = 1 - (lax.shift_right_logical(word, (tile % 2) * 15 + slot) & 1)
                    rhs.append(jnp.concatenate([top, top, low, ones], axis=0))
                    q = table_ref[where, 32:48, lanes]
                    sums.append(jnp.where(alive == 1, q, jnp.zeros_like(q)))
                rhs = jnp.concatenate(rhs, axis=1)
                sums = jnp.concatenate(sums, axis=1)
                both = jnp.dot(lhs, rhs, preferred_element_type=f32)
                stretch = both[:TILE]
                pull = both[TILE:] * jnp.exp2(stretch) / stretch
                high = pull.astype(bf16)
                low = (pull - high.astype(f32)).astype(bf16)
                dims = (((1,), (1,)), ((), ()))
                part = lax.dot_general(sums, high, dims, preferred_element_type=f32)
                part += lax.dot_general(sums, low, dims, preferred_element_type=f32)
                acc = part if acc is None else acc + part
            acc = acc[0:8] + acc[8:16]
            lanes = pl.ds(pl.multiple_of(tile * TILE, TILE), TILE)
            if not first:
                acc += before_ref[:, lanes]
            out_ref[:, lanes] = acc
            return carry

        lax.fori_loop(0, lhs_ref.shape[0], one_tile, 0, unroll=UNROLL)

    return kernel


def stage(names, flags, lhs, blocks, before, slots):
    first = before is None
    points = blocks[0].shape[1]
    smem = pl.BlockSpec(memory_space=pltpu.SMEM)
    vmem = pl.BlockSpec(memory_space=pltpu.VMEM)
    args = [names, flags, lhs, *blocks] + ([] if first else [before])
    return pl.pallas_call(
        make_stage_kernel(slots, first),
        out_shape=jax.ShapeDtypeStruct((8, points), f32),
        in_specs=[smem, smem] + [vmem] * (len(args) - 2),
        out_specs=vmem,
        scratch_shapes=[pltpu.VMEM((len(blocks), 48, points), bf16)],
        name="bond_stage",
        cost_estimate=pl.CostEstimate(flops=20_000_000_000, transcendentals=0, bytes_accessed=6_000_000),
    )(*args)


def finish_force(sums, field):
    now = field[0:3] + field[3:6]
    whole = 1.0 - field[6:7]
    inner = sums[0:3] - now * sums[6:7]
    outer = sums[3:6] - now * sums[7:8]
    return force_scale * whole * (field[7:8] * inner + outer)


def shift_layer(value, by):
    size = lax.axis_size("layer")
    pairs = [(i, i + by) for i in range(size) if 0 <= i + by < size]
    return lax.ppermute(value, "layer", pairs)


def shift_sector(value, by):
    size = lax.axis_size("blk")
    return lax.ppermute(value, "blk", [(i, (i + by) % size) for i in range(size)])


def layered(value):
    return [shift_layer(value, 1), value, shift_layer(value, -1)]


def on_device(
    ref_pos,
    disk_disp,
    disk_vel,
    damage,
    modulus,
    body_load,
    nbr_tiles,
    break_flags,
    blade_disp,
    blade_vel,
    elem_nodes,
    elem_modulus,
    elem_stiff,
    root_nodes,
    rim_points,
):
    disk_now = disk_disp[0, 0]
    blade_now = blade_disp[0, 0]
    field = jnp.concatenate([ref_pos[0, 0], disk_now, damage[0], modulus[0]], axis=0)
    names = nbr_tiles[0, 0]
    flags = break_flags[0, 0]
    behind = shift_sector(field, 1)
    ahead = shift_sector(field, -1)
    near = layered(field)
    far_behind = shift_sector(behind, 1)
    far_ahead = shift_sector(ahead, -1)
    rim_flat = rim_points[0, 0].reshape(-1)
    root_flat = root_nodes[0, 0].reshape(-1)
    rim_values = disk_now[:, rim_flat]
    root_values = blade_now[:, root_flat]
    swapped = lax.all_to_all(
        jnp.concatenate([rim_values, root_values], axis=0), "blk", split_axis=1, concat_axis=1, tiled=True
    )
    middle = layered(behind) + layered(ahead)
    outer = layered(far_behind) + layered(far_ahead)
    lhs = own_table(field)
    sums = stage(names, flags, lhs, near, None, (6, 7, 8))
    sums = stage(names, flags, lhs, middle, sums, (3, 4, 5, 9, 10, 11))
    sums = stage(names, flags, lhs, outer, sums, (0, 1, 2, 12, 13, 14))
    bond_force = finish_force(sums, field)
    loads = spring * (swapped[0:3] - root_values)
    coupling = jnp.zeros_like(blade_now).at[:, root_flat].add(loads)
    returned = spring * (rim_values - swapped[3:6])
    reaction = jnp.zeros_like(disk_now).at[:, rim_flat].add(-returned)
    connect = elem_nodes[0, 0]
    elem_count = connect.shape[1]
    gathered = blade_now[:, connect].reshape(24, elem_count)
    elem_force = elem_modulus[0, 0][None, :] * jnp.dot(
        elem_stiff, gathered, precision=lax.Precision.HIGHEST, preferred_element_type=jnp.float32
    )
    internal = jnp.zeros_like(blade_now).at[:, connect.reshape(-1)].add(-elem_force.reshape(3, -1))
    disk_vel_new = disk_vel[0, 0] + time_step * (bond_force + body_load[0, 0] + reaction)
    disk_disp_new = disk_now + time_step * disk_vel_new
    blade_vel_new = blade_vel[0, 0] + time_step * (internal + coupling)
    blade_disp_new = blade_now + time_step * blade_vel_new
    return (
        disk_disp_new[None, None],
        disk_vel_new[None, None],
        blade_disp_new[None, None],
        blade_vel_new[None, None],
    )


def solution(mesh):
    in_specs = (
        P("blk", "layer", None, None),
        P("blk", "layer", None, None),
        P("blk", "layer", None, None),
        P("blk", "layer", None),
        P("blk", "layer", None),
        P("blk", "layer", None, None),
        P("blk", "layer", None, None),
        P("blk", "layer", None),
        P("blk", "layer", None, None),
        P("blk", "layer", None, None),
        P("blk", "layer", None, None),
        P("blk", "layer", None),
        P(),
        P("blk", "layer", None, None),
        P("blk", "layer", None, None),
    )
    out_specs = (
        P("blk", "layer", None, None),
        P("blk", "layer", None, None),
        P("blk", "layer", None, None),
        P("blk", "layer", None, None),
    )
    return jax.shard_map(
        on_device, mesh=mesh, in_specs=in_specs, out_specs=out_specs, check_vma=False
    )
```

```python
import math
import jax
import jax.numpy as jnp
from jax import lax
from jax.experimental import pallas as pl
from jax.experimental.pallas import tpu as pltpu
from jax.sharding import PartitionSpec as P

TILE = 128
log_scale = math.log2(math.e) / 9.0
force_scale = -0.125 * log_scale * math.exp(1.0 / 9.0)
f32 = jnp.float32
bf16 = jnp.bfloat16
UNROLL = 8
UNROLL_OTHER = 8
OWN_GROUP = 2
own_slots = (1, 4, 7, 10, 13)
other_slots = (0, 2, 3, 5, 6, 8, 9, 11, 12, 14)
OWN_UNROLL = 4
spring = 0.5
time_step = 0.5


def split3(value):
    high = value.astype(bf16).astype(f32)
    rest = value - high
    middle = rest.astype(bf16).astype(f32)
    return high, middle, (rest - middle)


def point_terms(v):
    row = lax.broadcasted_iota(jnp.int32, v.shape, 0)
    disp = pltpu.roll(v, 5, 0)
    now = v + disp
    first = row < 3
    ref_norm = jnp.sum(jnp.where(first, v * v, 0.0), axis=0, keepdims=True)
    growth = jnp.sum(jnp.where(first, disp * (v + now), 0.0), axis=0, keepdims=True)
    return row, disp, now, ref_norm, growth


def own_kernel(field_ref, lhs_ref):
    def one_tile(tile, carry):
        v = field_ref[:, pl.ds(pl.multiple_of(tile * TILE, TILE), TILE)]
        row, disp, now, ref_norm, growth = point_terms(v)
        row16 = lax.broadcasted_iota(jnp.int32, (16, TILE), 0)
        coef_ref = jnp.where(row < 3, 2.0 * log_scale * v, jnp.where(row == 6, -log_scale, 0.0))
        coef_now = jnp.where(
            row < 3,
            -2.0 * disp,
            jnp.where(row < 6, -2.0 * pltpu.roll(now, 3, 0), jnp.where(row == 7, 1.0, 0.0)),
        )
        for place, coef, alone in (
            (0, coef_ref, -log_scale * (1.0 + ref_norm)),
            (1, coef_now, growth),
        ):
            high, middle, low = split3(coef)
            a, b, c = split3(alone)
            const = jnp.where(row16 == 0, a, jnp.where(row16 == 1, b, jnp.where(row16 == 2, c, 0.0)))
            rows = jnp.concatenate([high, high, middle, middle, high, low, const], axis=0)
            lhs_ref[tile, pl.ds(place * TILE, TILE), :] = rows.T.astype(bf16)
        return carry

    lax.fori_loop(0, field_ref.shape[1] // TILE, one_tile, 0, unroll=OWN_UNROLL)


def own_table(field):
    tiles = field.shape[1] // TILE
    return pl.pallas_call(
        own_kernel,
        out_shape=jax.ShapeDtypeStruct((tiles, 2 * TILE, 64), bf16),
        name="own_table",
        cost_estimate=pl.CostEstimate(flops=8_000_000_000, transcendentals=0, bytes_accessed=4_500_000),
    )(field)


def fill_table(field_ref, table_ref, row_start, place, chunk):
    def one(step, carry):
        lanes = pl.ds(pl.multiple_of(step * chunk, chunk), chunk)
        v = field_ref[row_start : row_start + 8, lanes]
        row, disp, now, ref_norm, growth = point_terms(v)
        terms = jnp.where(row < 6, v, jnp.where(row == 6, ref_norm, growth))
        high, middle, low = split3(terms)
        table_ref[place, 0:16, lanes] = jnp.concatenate([high, middle], axis=0).astype(bf16)
        table_ref[place, 16:32, lanes] = jnp.concatenate([low, high], axis=0).astype(bf16)
        whole = 1.0 - v[6:7]
        stiff = v[7:8]
        spread = jnp.where(row < 3, now, jnp.where(row < 6, pltpu.roll(now, 3, 0), 1.0))
        weight = whole * jnp.where((row < 3) | (row == 6), 1.0, stiff)
        sums = spread * weight
        q_high = sums.astype(bf16).astype(f32)
        table_ref[place, 32:48, lanes] = jnp.concatenate([q_high, sums - q_high], axis=0).astype(bf16)
        return carry

    lax.fori_loop(0, field_ref.shape[1] // chunk, one, 0)


def pair_sums(tile, slots, table_ref, names_ref, word, lhs, group):
    ones = jnp.ones((16, TILE), bf16)
    acc = None
    for start in range(0, len(slots), group):
        rhs, sums = [], []
        for place in range(start, min(start + group, len(slots))):
            slot = slots[place]
            name = names_ref[tile, slot]
            lanes = pl.ds(pl.multiple_of((name % 64) * TILE, TILE), TILE)
            top = table_ref[place, 0:16, lanes]
            low = table_ref[place, 16:32, lanes]
            alive = 1 - (lax.shift_right_logical(word, (tile % 2) * 15 + slot) & 1)
            rhs.append(jnp.concatenate([top, top, low, ones], axis=0))
            q = table_ref[place, 32:48, lanes]
            sums.append(jnp.where(alive == 1, q, jnp.zeros_like(q)))
        while len(rhs) < group:
            rhs.append(rhs[-1])
            sums.append(jnp.zeros_like(sums[-1]))
        rhs = jnp.concatenate(rhs, axis=1)
        sums = jnp.concatenate(sums, axis=1)
        both = jnp.dot(lhs, rhs, preferred_element_type=f32)
        stretch = both[:TILE]
        pull = both[TILE:] * jnp.exp2(stretch) / stretch
        high = pull.astype(bf16)
        low = (pull - high.astype(f32)).astype(bf16)
        dims = (((1,), (1,)), ((), ()))
        part = lax.dot_general(sums, high, dims, preferred_element_type=f32)
        part += lax.dot_general(sums, low, dims, preferred_element_type=f32)
        acc = part if acc is None else acc + part
    return acc[0:8] + acc[8:16]


def own_layer_kernel(names_ref, flags_ref, lhs_ref, *refs):
    out_ref, table_ref = refs[-2:]
    for place, ref in enumerate(refs[:-2]):
        fill_table(ref, table_ref, 0, place, 512)

    def one_tile(tile, carry):
        lanes = pl.ds(pl.multiple_of(tile * TILE, TILE), TILE)
        word = flags_ref[tile // 2]
        out_ref[:, lanes] = pair_sums(
            tile, own_slots, table_ref, names_ref, word, lhs_ref[tile], OWN_GROUP
        )
        return carry

    lax.fori_loop(0, lhs_ref.shape[0], one_tile, 0, unroll=UNROLL)


def other_layer_kernel(
    names_ref, flags_ref, layer_ref, lhs_ref, below_ref, own_ref, above_ref,
    sums_ref, vel_ref, body_ref, react_ref, disp_out_ref, vel_out_ref, table_ref,
):
    layer = layer_ref[0]
    for side, ref, edge in ((0, below_ref, 0), (1, above_ref, 3)):

        @pl.when(layer == edge)
        def _():
            for sector in range(5):
                fill_table(own_ref, table_ref, sector * 8, sector * 2 + side, 512)

        @pl.when(layer != edge)
        def _():
            for sector in range(5):
                fill_table(ref, table_ref, sector * 8, sector * 2 + side, 512)

    def one_tile(tile, carry):
        lanes = pl.ds(pl.multiple_of(tile * TILE, TILE), TILE)
        word = flags_ref[tile // 2]
        acc = pair_sums(tile, other_slots, table_ref, names_ref, word, lhs_ref[tile], 2)
        acc += sums_ref[:, lanes]
        own = own_ref[16:24, lanes]
        disp = own[3:6]
        now = own[0:3] + disp
        whole = 1.0 - own[6:7]
        inner = acc[0:3] - now * acc[6:7]
        outer = acc[3:6] - now * acc[7:8]
        force = force_scale * whole * (own[7:8] * inner + outer)
        vel = vel_ref[:, lanes] + time_step * (force + body_ref[:, lanes] + react_ref[:, lanes])
        vel_out_ref[:, lanes] = vel
        disp_out_ref[:, lanes] = disp + time_step * vel
        return carry

    lax.fori_loop(0, lhs_ref.shape[0], one_tile, 0, unroll=UNROLL_OTHER)


def cost(flops):
    return pl.CostEstimate(flops=flops, transcendentals=0, bytes_accessed=6_000_000)


smem = pl.BlockSpec(memory_space=pltpu.SMEM)
vmem = pl.BlockSpec(memory_space=pltpu.VMEM)


def own_layer_sums(names, flags, lhs, blocks):
    points = blocks[0].shape[1]
    return pl.pallas_call(
        own_layer_kernel,
        out_shape=jax.ShapeDtypeStruct((8, points), f32),
        in_specs=[smem, smem] + [vmem] * (1 + len(blocks)),
        out_specs=vmem,
        scratch_shapes=[pltpu.VMEM((len(blocks), 48, points), bf16)],
        name="own_layer",
        cost_estimate=cost(18_000_000_000),
    )(names, flags, lhs, *blocks)


def other_layer_update(names, flags, layer, lhs, below, own, above, sums, vel, body, react):
    points = own.shape[1]
    shape = jax.ShapeDtypeStruct((3, points), f32)
    return pl.pallas_call(
        other_layer_kernel,
        out_shape=(shape, shape),
        in_specs=[smem] * 3 + [vmem] * 8,
        out_specs=(vmem, vmem),
        scratch_shapes=[pltpu.VMEM((10, 48, points), bf16)],
        name="other_layer",
        cost_estimate=cost(36_000_000_000),
    )(names, flags, layer, lhs, below, own, above, sums, vel, body, react)


def parts32(value):
    high, middle, low = split3(value)
    return jnp.concatenate([high, middle, low, jnp.zeros_like(low)], axis=0)


def join32(value):
    return value[0:8] + value[8:16] + value[16:24]


def one_hot(index, count):
    row = lax.broadcasted_iota(jnp.int32, (count, index.shape[1]), 0)
    return jnp.where(row == index, 1.0, 0.0).astype(bf16)


across = (((1,), (1,)), ((), ()))


def values_kernel(field_ref, blade_ref, rim_ref, root_ref, out_ref, pad_ref):
    rim = rim_ref[...]
    tile_of = lax.shift_right_logical(rim, 7)
    lane_hot = one_hot(rim & 127, TILE)

    def one_batch(step, acc):
        rows = []
        for inner in range(8):
            start = pl.multiple_of(step * (8 * TILE) + inner * TILE, TILE)
            rows.append(parts32(field_ref[:, pl.ds(start, TILE)]))
        found = jnp.dot(jnp.concatenate(rows, axis=0).astype(bf16), lane_hot, preferred_element_type=f32)
        for inner in range(8):
            acc = acc + jnp.where(tile_of == step * 8 + inner, found[inner * 32 : inner * 32 + 24], 0.0)
        return acc

    acc = lax.fori_loop(0, field_ref.shape[1] // (8 * TILE), one_batch, jnp.zeros((24, rim.shape[1]), f32))
    out_ref[0:3] = join32(acc)[3:6]
    pad_ref[...] = jnp.zeros_like(pad_ref)
    pad_ref[0:3] = blade_ref[...]
    found = jnp.dot(
        parts32(pad_ref[...]).astype(bf16), one_hot(root_ref[...], blade_ref.shape[1]), preferred_element_type=f32
    )
    out_ref[3:6] = join32(found)[0:3]


def coupling_values(field, blade, rim, root):
    return pl.pallas_call(
        values_kernel,
        out_shape=jax.ShapeDtypeStruct((6, rim.shape[1]), f32),
        scratch_shapes=[pltpu.VMEM((8, blade.shape[1]), f32)],
        name="coupling_values",
        cost_estimate=cost(3_000_000_000),
    )(field, blade, rim, root)


def coupling_kernel(
    swapped_ref, sent_ref, rim_ref, root_ref, nodes_ref, scale_ref, stiff_ref, blade_ref, vel_ref,
    react_ref, disp_out_ref, vel_out_ref, pad_ref, elem_ref,
):
    nodes = blade_ref.shape[1]
    rim = rim_ref[...]
    tile_of = lax.shift_right_logical(rim, 7)
    lane_hot = one_hot(rim & 127, TILE)
    pad_ref[...] = jnp.zeros_like(pad_ref)
    pad_ref[0:3] = spring * (swapped_ref[3:6] - sent_ref[0:3])
    back = parts32(pad_ref[...])

    def one_batch(step, carry):
        rows = jnp.concatenate(
            [jnp.where(tile_of == step * 8 + inner, back, 0.0) for inner in range(8)], axis=0
        )
        put = lax.dot_general(rows.astype(bf16), lane_hot, across, preferred_element_type=f32)
        for inner in range(8):
            start = pl.multiple_of(step * (8 * TILE) + inner * TILE, TILE)
            react_ref[:, pl.ds(start, TILE)] = join32(put[inner * 32 : inner * 32 + 32])[0:3]
        return carry

    lax.fori_loop(0, react_ref.shape[1] // (8 * TILE), one_batch, 0)
    pad_ref[0:3] = spring * (swapped_ref[0:3] - sent_ref[3:6])
    loads = parts32(pad_ref[...]).astype(bf16)
    coupling = join32(
        lax.dot_general(loads, one_hot(root_ref[...], nodes), across, preferred_element_type=f32)
    )
    pad_ref[0:3] = blade_ref[...]
    blade = parts32(pad_ref[...]).astype(bf16)
    hots = []
    for q in range(8):
        hot = one_hot(nodes_ref[q : q + 1], nodes)
        hots.append(hot)
        taken = join32(jnp.dot(blade, hot, preferred_element_type=f32))
        for a in range(3):
            elem_ref[8 * a + q : 8 * a + q + 1, :] = taken[a : a + 1]
    force = scale_ref[...] * jnp.dot(
        stiff_ref[...], elem_ref[...], precision=lax.Precision.HIGHEST, preferred_element_type=f32
    )
    high, middle, low = split3(force)
    force = jnp.concatenate([high, middle, low, jnp.zeros((8, force.shape[1]), f32)], axis=0).astype(bf16)
    row = lax.broadcasted_iota(jnp.int32, (24, nodes), 0)
    total = jnp.zeros((24, nodes), f32)
    for q in range(8):
        put = lax.dot_general(force, hots[q], across, preferred_element_type=f32)
        total = total + jnp.where(row % 8 == q, put[0:24] + put[24:48] + put[48:72], 0.0)
    for a in range(3):
        internal = -jnp.sum(total[8 * a : 8 * a + 8], axis=0, keepdims=True)
        vel = vel_ref[a : a + 1] + time_step * (internal + coupling[a : a + 1])
        vel_out_ref[a : a + 1] = vel
        disp_out_ref[a : a + 1] = blade_ref[a : a + 1] + time_step * vel


def coupling_update(swapped, sent, rim, root, nodes, scale, stiff, blade, vel, points):
    small = jax.ShapeDtypeStruct(blade.shape, f32)
    return pl.pallas_call(
        coupling_kernel,
        out_shape=(jax.ShapeDtypeStruct((3, points), f32), small, small),
        scratch_shapes=[
            pltpu.VMEM((8, blade.shape[1]), f32),
            pltpu.VMEM((24, nodes.shape[1]), f32),
        ],
        name="coupling_update",
        cost_estimate=cost(4_000_000_000),
    )(swapped, sent, rim, root, nodes, scale, stiff, blade, vel)


def shift_layer(value, by):
    size = lax.axis_size("layer")
    pairs = [(i, i + by) for i in range(size) if 0 <= i + by < size]
    return lax.ppermute(value, "layer", pairs)


def shift_sector(value, by):
    size = lax.axis_size("blk")
    return lax.ppermute(value, "blk", [(i, (i + by) % size) for i in range(size)])


def on_device(
    ref_pos,
    disk_disp,
    disk_vel,
    damage,
    modulus,
    body_load,
    nbr_tiles,
    break_flags,
    blade_disp,
    blade_vel,
    elem_nodes,
    elem_modulus,
    elem_stiff,
    root_nodes,
    rim_points,
):
    disk_now = disk_disp[0, 0]
    blade_now = blade_disp[0, 0]
    field = jnp.concatenate([ref_pos[0, 0], disk_now, damage[0], modulus[0]], axis=0)
    names = nbr_tiles[0, 0]
    flags = break_flags[0, 0]
    far_behind = shift_sector(field, 2)
    behind = shift_sector(field, 1)
    ahead = shift_sector(field, -1)
    far_ahead = shift_sector(field, -2)
    rim = rim_points[0, 0].reshape(1, -1)
    root = root_nodes[0, 0].reshape(1, -1)
    sent = coupling_values(field, blade_now, rim, root)
    swapped = lax.all_to_all(sent, "blk", split_axis=1, concat_axis=1, tiled=True)
    lhs = own_table(field)
    blocks = [far_behind, behind, field, ahead, far_ahead]
    own = jnp.concatenate(blocks, axis=0)
    below = shift_layer(own, 1)
    above = shift_layer(own, -1)
    sums = own_layer_sums(names, flags, lhs, blocks)
    reaction, blade_disp_new, blade_vel_new = coupling_update(
        swapped, sent, rim, root, elem_nodes[0, 0], elem_modulus[0], elem_stiff, blade_now,
        blade_vel[0, 0], field.shape[1],
    )
    layer = lax.axis_index("layer").reshape(1).astype(jnp.int32)
    disk_disp_new, disk_vel_new = other_layer_update(
        names, flags, layer, lhs, below, own, above, sums, disk_vel[0, 0], body_load[0, 0], reaction
    )
    return (
        disk_disp_new[None, None],
        disk_vel_new[None, None],
        blade_disp_new[None, None],
        blade_vel_new[None, None],
    )


def solution(mesh):
    in_specs = (
        P("blk", "layer", None, None),
        P("blk", "layer", None, None),
        P("blk", "layer", None, None),
        P("blk", "layer", None),
        P("blk", "layer", None),
        P("blk", "layer", None, None),
        P("blk", "layer", None, None),
        P("blk", "layer", None),
        P("blk", "layer", None, None),
        P("blk", "layer", None, None),
        P("blk", "layer", None, None),
        P("blk", "layer", None),
        P(),
        P("blk", "layer", None, None),
        P("blk", "layer", None, None),
    )
    out_specs = (
        P("blk", "layer", None, None),
        P("blk", "layer", None, None),
        P("blk", "layer", None, None),
        P("blk", "layer", None, None),
    )
    return jax.shard_map(
        on_device, mesh=mesh, in_specs=in_specs, out_specs=out_specs, check_vma=False
    )
```

```python
import math
import jax
import jax.numpy as jnp
from jax import lax
from jax.experimental import pallas as pl
from jax.experimental.pallas import tpu as pltpu
from jax.sharding import PartitionSpec as P

TILE = 128
log_scale = math.log2(math.e) / 9.0
force_scale = -0.125 * log_scale * math.exp(1.0 / 9.0)
f32 = jnp.float32
bf16 = jnp.bfloat16
UNROLL = 16
UNROLL_OTHER = 8
OWN_GROUP = 2
own_slots = (1, 4, 7, 10, 13)
other_slots = (0, 2, 3, 5, 6, 8, 9, 11, 12, 14)
OWN_UNROLL = 4
spring = 0.5
time_step = 0.5


def split3(value):
    high = value.astype(bf16).astype(f32)
    rest = value - high
    middle = rest.astype(bf16).astype(f32)
    return high, middle, (rest - middle)


def point_terms(v):
    row = lax.broadcasted_iota(jnp.int32, v.shape, 0)
    disp = pltpu.roll(v, 5, 0)
    now = v + disp
    first = row < 3
    ref_norm = jnp.sum(jnp.where(first, v * v, 0.0), axis=0, keepdims=True)
    growth = jnp.sum(jnp.where(first, disp * (v + now), 0.0), axis=0, keepdims=True)
    return row, disp, now, ref_norm, growth


def own_kernel(field_ref, lhs_ref):
    def one_tile(tile, carry):
        v = field_ref[:, pl.ds(pl.multiple_of(tile * TILE, TILE), TILE)]
        row, disp, now, ref_norm, growth = point_terms(v)
        row16 = lax.broadcasted_iota(jnp.int32, (16, TILE), 0)
        coef_ref = jnp.where(row < 3, 2.0 * log_scale * v, jnp.where(row == 6, -log_scale, 0.0))
        coef_now = jnp.where(
            row < 3,
            -2.0 * disp,
            jnp.where(row < 6, -2.0 * pltpu.roll(now, 3, 0), jnp.where(row == 7, 1.0, 0.0)),
        )
        for place, coef, alone in (
            (0, coef_ref, -log_scale * (1.0 + ref_norm)),
            (1, coef_now, growth),
        ):
            high, middle, low = split3(coef)
            a, b, c = split3(alone)
            const = jnp.where(row16 == 0, a, jnp.where(row16 == 1, b, jnp.where(row16 == 2, c, 0.0)))
            rows = jnp.concatenate([high, high, middle, middle, high, low, const], axis=0)
            lhs_ref[tile, pl.ds(place * TILE, TILE), :] = rows.T.astype(bf16)
        return carry

    lax.fori_loop(0, field_ref.shape[1] // TILE, one_tile, 0, unroll=OWN_UNROLL)


def own_table(field):
    tiles = field.shape[1] // TILE
    return pl.pallas_call(
        own_kernel,
        out_shape=jax.ShapeDtypeStruct((tiles, 2 * TILE, 64), bf16),
        name="own_table",
        cost_estimate=pl.CostEstimate(flops=8_000_000_000, transcendentals=0, bytes_accessed=4_500_000),
    )(field)


def fill_table(field_ref, table_ref, row_start, place, chunk):
    def one(step, carry):
        lanes = pl.ds(pl.multiple_of(step * chunk, chunk), chunk)
        v = field_ref[row_start : row_start + 8, lanes]
        row, disp, now, ref_norm, growth = point_terms(v)
        terms = jnp.where(row < 6, v, jnp.where(row == 6, ref_norm, growth))
        high, middle, low = split3(terms)
        table_ref[place, 0:16, lanes] = jnp.concatenate([high, middle], axis=0).astype(bf16)
        table_ref[place, 16:32, lanes] = jnp.concatenate([low, high], axis=0).astype(bf16)
        whole = 1.0 - v[6:7]
        stiff = v[7:8]
        spread = jnp.where(row < 3, now, jnp.where(row < 6, pltpu.roll(now, 3, 0), 1.0))
        weight = whole * jnp.where((row < 3) | (row == 6), 1.0, stiff)
        sums = spread * weight
        q_high = sums.astype(bf16).astype(f32)
        table_ref[place, 32:48, lanes] = jnp.concatenate([q_high, sums - q_high], axis=0).astype(bf16)
        return carry

    lax.fori_loop(0, field_ref.shape[1] // chunk, one, 0)


def pair_sums(tile, slots, table_ref, names_ref, word, lhs, group):
    ones = jnp.ones((16, TILE), bf16)
    acc = None
    for start in range(0, len(slots), group):
        rhs, sums = [], []
        for place in range(start, min(start + group, len(slots))):
            slot = slots[place]
            name = names_ref[slot, tile]
            lanes = pl.ds(pl.multiple_of((name % 64) * TILE, TILE), TILE)
            top = table_ref[place, 0:16, lanes]
            low = table_ref[place, 16:32, lanes]
            alive = 1 - (lax.shift_right_logical(word, (tile % 2) * 15 + slot) & 1)
            rhs.append(jnp.concatenate([top, top, low, ones], axis=0))
            q = table_ref[place, 32:48, lanes]
            sums.append(jnp.where(alive == 1, q, jnp.zeros_like(q)))
        while len(rhs) < group:
            rhs.append(rhs[-1])
            sums.append(jnp.zeros_like(sums[-1]))
        rhs = jnp.concatenate(rhs, axis=1)
        sums = jnp.concatenate(sums, axis=1)
        both = jnp.dot(lhs, rhs, preferred_element_type=f32)
        stretch = both[:TILE]
        pull = both[TILE:] * jnp.exp2(stretch) / stretch
        high = pull.astype(bf16)
        low = (pull - high.astype(f32)).astype(bf16)
        dims = (((1,), (1,)), ((), ()))
        part = lax.dot_general(sums, high, dims, preferred_element_type=f32)
        part += lax.dot_general(sums, low, dims, preferred_element_type=f32)
        acc = part if acc is None else acc + part
    return acc[0:8] + acc[8:16]


def own_layer_kernel(names_ref, flags_ref, lhs_ref, *refs):
    out_ref, table_ref = refs[-2:]
    for place, ref in enumerate(refs[:-2]):
        fill_table(ref, table_ref, 0, place, 512)

    def one_tile(tile, carry):
        lanes = pl.ds(pl.multiple_of(tile * TILE, TILE), TILE)
        word = flags_ref[tile // 2]
        out_ref[:, lanes] = pair_sums(
            tile, own_slots, table_ref, names_ref, word, lhs_ref[tile], OWN_GROUP
        )
        return carry

    lax.fori_loop(0, lhs_ref.shape[0], one_tile, 0, unroll=UNROLL)


def other_layer_kernel(
    names_ref, flags_ref, layer_ref, lhs_ref, below_ref, own_ref, above_ref,
    sums_ref, vel_ref, body_ref, react_ref, disp_out_ref, vel_out_ref, table_ref,
):
    layer = layer_ref[0]
    for side, ref, edge in ((0, below_ref, 0), (1, above_ref, 3)):

        @pl.when(layer == edge)
        def _():
            for sector in range(5):
                fill_table(own_ref, table_ref, sector * 8, sector * 2 + side, 512)

        @pl.when(layer != edge)
        def _():
            for sector in range(5):
                fill_table(ref, table_ref, sector * 8, sector * 2 + side, 512)

    def one_tile(tile, carry):
        lanes = pl.ds(pl.multiple_of(tile * TILE, TILE), TILE)
        word = flags_ref[tile // 2]
        acc = pair_sums(tile, other_slots, table_ref, names_ref, word, lhs_ref[tile], 2)
        acc += sums_ref[:, lanes]
        own = own_ref[16:24, lanes]
        disp = own[3:6]
        now = own[0:3] + disp
        whole = 1.0 - own[6:7]
        inner = acc[0:3] - now * acc[6:7]
        outer = acc[3:6] - now * acc[7:8]
        force = force_scale * whole * (own[7:8] * inner + outer)
        force += react_ref[:, lanes]
        for c in range(3):
            load = force[c : c + 1] + body_ref[c, :, lanes]
            vel = vel_ref[c, :, lanes] + time_step * load
            vel_out_ref[c, :, lanes] = vel
            disp_out_ref[c, :, lanes] = disp[c : c + 1] + time_step * vel
        return carry

    lax.fori_loop(0, lhs_ref.shape[0], one_tile, 0, unroll=UNROLL_OTHER)


def cost(flops):
    return pl.CostEstimate(flops=flops, transcendentals=0, bytes_accessed=6_000_000)


smem = pl.BlockSpec(memory_space=pltpu.SMEM)
vmem = pl.BlockSpec(memory_space=pltpu.VMEM)


def own_layer_sums(names, flags, lhs, blocks):
    points = blocks[0].shape[1]
    return pl.pallas_call(
        own_layer_kernel,
        out_shape=jax.ShapeDtypeStruct((8, points), f32),
        in_specs=[smem, smem] + [vmem] * (1 + len(blocks)),
        out_specs=vmem,
        scratch_shapes=[pltpu.VMEM((len(blocks), 48, points), bf16)],
        name="own_layer",
        cost_estimate=cost(18_000_000_000),
    )(names, flags, lhs, *blocks)


def other_layer_update(names, flags, layer, lhs, below, own, above, sums, vel, body, react):
    points = own.shape[1]
    shape = jax.ShapeDtypeStruct((3, 1, points), f32)
    return pl.pallas_call(
        other_layer_kernel,
        out_shape=(shape, shape),
        in_specs=[smem] * 3 + [vmem] * 8,
        out_specs=(vmem, vmem),
        scratch_shapes=[pltpu.VMEM((10, 48, points), bf16)],
        name="other_layer",
        cost_estimate=cost(36_000_000_000),
    )(names, flags, layer, lhs, below, own, above, sums, vel, body, react)


def parts32(value):
    high, middle, low = split3(value)
    return jnp.concatenate([high, middle, low, jnp.zeros_like(low)], axis=0)


def join32(value):
    return value[0:8] + value[8:16] + value[16:24]


def one_hot(index, count):
    row = lax.broadcasted_iota(jnp.int32, (count, index.shape[1]), 0)
    return jnp.where(row == index, 1.0, 0.0).astype(bf16)


def slot_row(index_ref):
    return jnp.concatenate([index_ref[c : c + 1, :] for c in range(index_ref.shape[0])], axis=1)


across = (((1,), (1,)), ((), ()))


def values_kernel(field_ref, blade_ref, rim_ref, root_ref, out_ref, pad_ref):
    rim = slot_row(rim_ref)
    root = slot_row(root_ref)
    tile_of = lax.shift_right_logical(rim, 7)
    lane_hot = one_hot(rim & 127, TILE)

    def one_batch(step, acc):
        rows = []
        for inner in range(8):
            start = pl.multiple_of(step * (8 * TILE) + inner * TILE, TILE)
            rows.append(parts32(field_ref[:, pl.ds(start, TILE)]))
        found = jnp.dot(jnp.concatenate(rows, axis=0).astype(bf16), lane_hot, preferred_element_type=f32)
        for inner in range(8):
            acc = acc + jnp.where(tile_of == step * 8 + inner, found[inner * 32 : inner * 32 + 24], 0.0)
        return acc

    acc = lax.fori_loop(0, field_ref.shape[1] // (8 * TILE), one_batch, jnp.zeros((24, rim.shape[1]), f32))
    out_ref[0:3] = join32(acc)[3:6]
    pad_ref[...] = jnp.zeros_like(pad_ref)
    for c in range(3):
        pad_ref[c : c + 1] = blade_ref[c]
    found = jnp.dot(
        parts32(pad_ref[...]).astype(bf16), one_hot(root, blade_ref.shape[2]), preferred_element_type=f32
    )
    out_ref[3:6] = join32(found)[0:3]


def coupling_values(field, blade, rim, root):
    return pl.pallas_call(
        values_kernel,
        out_shape=jax.ShapeDtypeStruct((6, rim.shape[0] * rim.shape[1]), f32),
        scratch_shapes=[pltpu.VMEM((8, blade.shape[2]), f32)],
        name="coupling_values",
        cost_estimate=cost(3_000_000_000),
    )(field, blade, rim, root)


def coupling_kernel(
    swapped_ref, sent_ref, rim_ref, root_ref, nodes_ref, scale_ref, stiff_ref, blade_ref, vel_ref,
    after_ref, react_ref, disp_out_ref, vel_out_ref, pad_ref, elem_ref,
):
    nodes = blade_ref.shape[2]
    rim = slot_row(rim_ref)
    root = slot_row(root_ref)
    tile_of = lax.shift_right_logical(rim, 7)
    lane_hot = one_hot(rim & 127, TILE)
    pad_ref[...] = jnp.zeros_like(pad_ref)
    pad_ref[0:3] = spring * (swapped_ref[3:6] - sent_ref[0:3])
    back = parts32(pad_ref[...])

    def one_batch(step, carry):
        rows = jnp.concatenate(
            [jnp.where(tile_of == step * 8 + inner, back, 0.0) for inner in range(8)], axis=0
        )
        put = lax.dot_general(rows.astype(bf16), lane_hot, across, preferred_element_type=f32)
        for inner in range(8):
            start = pl.multiple_of(step * (8 * TILE) + inner * TILE, TILE)
            react_ref[:, pl.ds(start, TILE)] = join32(put[inner * 32 : inner * 32 + 32])[0:3]
        return carry

    lax.fori_loop(0, react_ref.shape[1] // (8 * TILE), one_batch, 0)
    pad_ref[0:3] = spring * (swapped_ref[0:3] - sent_ref[3:6])
    loads = parts32(pad_ref[...]).astype(bf16)
    coupling = join32(
        lax.dot_general(loads, one_hot(root, nodes), across, preferred_element_type=f32)
    )
    for c in range(3):
        pad_ref[c : c + 1] = blade_ref[c]
    blade = parts32(pad_ref[...]).astype(bf16)
    hots = []
    for q in range(8):
        hot = one_hot(nodes_ref[q : q + 1], nodes)
        hots.append(hot)
        taken = join32(jnp.dot(blade, hot, preferred_element_type=f32))
        for a in range(3):
            elem_ref[8 * a + q : 8 * a + q + 1, :] = taken[a : a + 1]
    force = scale_ref[...] * jnp.dot(
        stiff_ref[...], elem_ref[...], precision=lax.Precision.HIGHEST, preferred_element_type=f32
    )
    high, middle, low = split3(force)
    force = jnp.concatenate([high, middle, low, jnp.zeros((8, force.shape[1]), f32)], axis=0).astype(bf16)
    row = lax.broadcasted_iota(jnp.int32, (24, nodes), 0)
    total = jnp.zeros((24, nodes), f32)
    for q in range(8):
        put = lax.dot_general(force, hots[q], across, preferred_element_type=f32)
        total = total + jnp.where(row % 8 == q, put[0:24] + put[24:48] + put[48:72], 0.0)
    for a in range(3):
        internal = -jnp.sum(total[8 * a : 8 * a + 8], axis=0, keepdims=True)
        vel = vel_ref[a] + time_step * (internal + coupling[a : a + 1])
        vel_out_ref[a] = vel
        disp_out_ref[a] = blade_ref[a] + time_step * vel


def coupling_update(swapped, sent, rim, root, nodes, scale, stiff, blade, vel, after, points):
    small = jax.ShapeDtypeStruct(blade.shape, f32)
    return pl.pallas_call(
        coupling_kernel,
        out_shape=(jax.ShapeDtypeStruct((3, points), f32), small, small),
        scratch_shapes=[
            pltpu.VMEM((8, blade.shape[2]), f32),
            pltpu.VMEM((24, nodes.shape[1]), f32),
        ],
        in_specs=[vmem] * 9 + [pl.BlockSpec(memory_space=pl.ANY)],
        name="coupling_update",
        cost_estimate=cost(4_000_000_000),
    )(swapped, sent, rim, root, nodes, scale, stiff, blade, vel, after)


def shift_layer(value, by):
    size = lax.axis_size("layer")
    pairs = [(i, i + by) for i in range(size) if 0 <= i + by < size]
    return lax.ppermute(value, "layer", pairs)


def shift_sector(value, by):
    size = lax.axis_size("blk")
    return lax.ppermute(value, "blk", [(i, (i + by) % size) for i in range(size)])


def on_device(
    ref_pos,
    disk_disp,
    disk_vel,
    damage,
    modulus,
    body_load,
    nbr_tiles,
    break_flags,
    blade_disp,
    blade_vel,
    elem_nodes,
    elem_modulus,
    elem_stiff,
    root_nodes,
    rim_points,
):
    disk_now = disk_disp[0, 0]
    field = jnp.concatenate([ref_pos[0, 0], disk_now, damage[0], modulus[0]], axis=0)
    names = nbr_tiles[0, 0].T
    flags = break_flags[0, 0]
    far_behind = shift_sector(field, 2)
    behind = shift_sector(field, 1)
    ahead = shift_sector(field, -1)
    far_ahead = shift_sector(field, -2)
    rim = rim_points[0, 0].T
    root = root_nodes[0, 0].T
    blade_rows = blade_disp.reshape(3, 1, -1)
    sent = coupling_values(field, blade_rows, rim, root)
    swapped = lax.all_to_all(
        sent.reshape(6, rim.shape[0], rim.shape[1]), "blk", split_axis=2, concat_axis=2, tiled=True
    )
    lhs = own_table(field)
    blocks = [far_behind, behind, field, ahead, far_ahead]
    own = jnp.concatenate(blocks, axis=0)
    below = shift_layer(own, 1)
    above = shift_layer(own, -1)
    sums = own_layer_sums(names, flags, lhs, blocks)
    swapped, sums = lax.optimization_barrier((swapped, sums))
    swapped = swapped.reshape(sent.shape)
    reaction, blade_disp_new, blade_vel_new = coupling_update(
        swapped, sent, rim, root, elem_nodes[0, 0], elem_modulus[0], elem_stiff, blade_rows,
        blade_vel.reshape(3, 1, -1), sums, field.shape[1],
    )
    layer = lax.axis_index("layer").reshape(1).astype(jnp.int32)
    disk_disp_new, disk_vel_new = other_layer_update(
        names, flags, layer, lhs, below, own, above, sums, disk_vel.reshape(3, 1, -1),
        body_load.reshape(3, 1, -1), reaction
    )
    return (
        disk_disp_new.reshape(disk_disp.shape),
        disk_vel_new.reshape(disk_vel.shape),
        blade_disp_new.reshape(blade_disp.shape),
        blade_vel_new.reshape(blade_vel.shape),
    )


def solution(mesh):
    in_specs = (
        P("blk", "layer", None, None),
        P("blk", "layer", None, None),
        P("blk", "layer", None, None),
        P("blk", "layer", None),
        P("blk", "layer", None),
        P("blk", "layer", None, None),
        P("blk", "layer", None, None),
        P("blk", "layer", None),
        P("blk", "layer", None, None),
        P("blk", "layer", None, None),
        P("blk", "layer", None, None),
        P("blk", "layer", None),
        P(),
        P("blk", "layer", None, None),
        P("blk", "layer", None, None),
    )
    out_specs = (
        P("blk", "layer", None, None),
        P("blk", "layer", None, None),
        P("blk", "layer", None, None),
        P("blk", "layer", None, None),
    )
    return jax.shard_map(
        on_device, mesh=mesh, in_specs=in_specs, out_specs=out_specs, check_vma=False
    )
```

```python
import math
import jax
import jax.numpy as jnp
from jax import lax
from jax.experimental import pallas as pl
from jax.experimental.pallas import tpu as pltpu
from jax.sharding import PartitionSpec as P

TILE = 128
log_scale = math.log2(math.e) / 9.0
force_scale = -0.125 * log_scale * math.exp(1.0 / 9.0)
f32 = jnp.float32
across = (((1,), (1,)), ((), ()))
bf16 = jnp.bfloat16
UNROLL = 16
UNROLL_OTHER = 8
own_slots = (1, 4, 7, 10, 13)
other_slots = (0, 2, 3, 5, 6, 8, 9, 11, 12, 14)
OWN_UNROLL = 8
spring = 0.5
time_step = 0.5


def split3(value):
    high = value.astype(bf16).astype(f32)
    rest = value - high
    middle = rest.astype(bf16).astype(f32)
    return high, middle, (rest - middle)


def point_terms(v):
    row = lax.broadcasted_iota(jnp.int32, v.shape, 0)
    disp = pltpu.roll(v, 5, 0)
    now = v + disp
    first = row < 3
    ref_norm = jnp.sum(jnp.where(first, v * v, 0.0), axis=0, keepdims=True)
    growth = jnp.sum(jnp.where(first, disp * (v + now), 0.0), axis=0, keepdims=True)
    return row, disp, now, ref_norm, growth


def own_kernel(field_ref, lhs_ref):
    def one_tile(tile, carry):
        v = field_ref[:, pl.ds(pl.multiple_of(tile * TILE, TILE), TILE)]
        row, disp, now, ref_norm, growth = point_terms(v)
        row16 = lax.broadcasted_iota(jnp.int32, (16, TILE), 0)
        coef_ref = jnp.where(row < 3, 2.0 * log_scale * v, jnp.where(row == 6, -log_scale, 0.0))
        coef_now = jnp.where(
            row < 3,
            -2.0 * disp,
            jnp.where(row < 6, -2.0 * pltpu.roll(now, 3, 0), jnp.where(row == 7, 1.0, 0.0)),
        )
        for place, coef, alone in (
            (0, coef_ref, -log_scale * (1.0 + ref_norm)),
            (1, coef_now, growth),
        ):
            high, middle, low = split3(coef)
            a, b, c = split3(alone)
            const = jnp.where(row16 == 0, a, jnp.where(row16 == 1, b, jnp.where(row16 == 2, c, 0.0)))
            rows = jnp.concatenate([high, high, middle, middle, high, low, const], axis=0)
            lhs_ref[tile, pl.ds(place * TILE, TILE), :] = rows.T.astype(bf16)
        return carry

    lax.fori_loop(0, field_ref.shape[1] // TILE, one_tile, 0, unroll=OWN_UNROLL)


def own_table(field):
    tiles = field.shape[1] // TILE
    return pl.pallas_call(
        own_kernel,
        out_shape=jax.ShapeDtypeStruct((tiles, 2 * TILE, 64), bf16),
        name="own_table",
        cost_estimate=pl.CostEstimate(flops=8_000_000_000, transcendentals=0, bytes_accessed=4_500_000),
    )(field)


def fill_table(field_ref, table_ref, row_start, place, chunk):
    def one(step, carry):
        lanes = pl.ds(pl.multiple_of(step * chunk, chunk), chunk)
        v = field_ref[row_start : row_start + 8, lanes]
        row = lax.broadcasted_iota(jnp.int32, v.shape, 0)
        now = v + pltpu.roll(v, 5, 0)
        grown = v * (v + jnp.where(row < 3, 0.0, 2.0 * pltpu.roll(v, 3, 0)))
        summed = grown + pltpu.roll(grown, 7, 0) + pltpu.roll(grown, 6, 0)
        terms = jnp.where(row < 6, v, jnp.where(row == 6, pltpu.roll(summed, 6, 0), pltpu.roll(summed, 4, 0)))
        high, middle, low = split3(terms)
        table_ref[place, 0:16, lanes] = jnp.concatenate([high, middle], axis=0).astype(bf16)
        table_ref[place, 16:32, lanes] = jnp.concatenate([low, high], axis=0).astype(bf16)
        whole = 1.0 - v[6:7]
        stiff = v[7:8]
        spread = jnp.where(row < 3, now, jnp.where(row < 6, pltpu.roll(now, 3, 0), 1.0))
        weight = whole * jnp.where((row < 3) | (row == 6), 1.0, stiff)
        sums = spread * weight
        q_high = sums.astype(bf16).astype(f32)
        table_ref[place, 32:48, lanes] = jnp.concatenate([q_high, sums - q_high], axis=0).astype(bf16)
        return carry

    lax.fori_loop(0, field_ref.shape[1] // chunk, one, 0)


def slot_terms(tile, slot, place, table_ref, names_ref, word):
    name = names_ref[slot, tile]
    lanes = pl.ds(pl.multiple_of((name % 64) * TILE, TILE), TILE)
    top = table_ref[place, 0:16, lanes]
    low = table_ref[place, 16:32, lanes]
    alive = 1 - (lax.shift_right_logical(word, (tile % 2) * 15 + slot) & 1)
    q = table_ref[place, 32:48, lanes]
    rhs = jnp.concatenate([top, top, low, jnp.ones((16, TILE), bf16)], axis=0)
    return rhs, jnp.where(alive == 1, q, jnp.zeros_like(q))


def pull_sums(lhs, rhs, sums):
    both = jnp.dot(lhs, rhs, preferred_element_type=f32)
    stretch = both[:TILE]
    pull = both[TILE:] * jnp.exp2(stretch) / stretch
    high = pull.astype(bf16)
    low = (pull - high.astype(f32)).astype(bf16)
    part = lax.dot_general(sums, high, across, preferred_element_type=f32)
    return part + lax.dot_general(sums, low, across, preferred_element_type=f32)


def pair_sums(tile, slots, table_ref, names_ref, word, lhs):
    acc = None
    for start in range(0, len(slots), 2):
        terms = [
            slot_terms(tile, slots[place], place, table_ref, names_ref, word) for place in (start, start + 1)
        ]
        part = pull_sums(
            lhs,
            jnp.concatenate([terms[0][0], terms[1][0]], axis=1),
            jnp.concatenate([terms[0][1], terms[1][1]], axis=1),
        )
        acc = part if acc is None else acc + part
    return acc


def own_layer_kernel(names_ref, flags_ref, lhs_ref, *refs):
    out_ref, table_ref = refs[-2:]
    for place, ref in enumerate(refs[:-2]):
        fill_table(ref, table_ref, 0, place, 512)

    last = len(own_slots) - 1

    def two_tiles(pair, carry):
        word = flags_ref[pair]
        tiles = (2 * pair, 2 * pair + 1)
        accs = [
            pair_sums(tile, own_slots[:last], table_ref, names_ref, word, lhs_ref[tile]) for tile in tiles
        ]
        terms = [slot_terms(tile, own_slots[last], last, table_ref, names_ref, word) for tile in tiles]
        none_rhs, none_sums = (jnp.zeros_like(part) for part in terms[0])
        rhs = jnp.concatenate(
            [
                jnp.concatenate([terms[0][0], none_rhs], axis=1),
                jnp.concatenate([none_rhs, terms[1][0]], axis=1),
            ],
            axis=0,
        )
        sums = jnp.concatenate(
            [
                jnp.concatenate([terms[0][1], none_sums], axis=1),
                jnp.concatenate([none_sums, terms[1][1]], axis=1),
            ],
            axis=0,
        )
        lhs = jnp.concatenate([lhs_ref[tiles[0]], lhs_ref[tiles[1]]], axis=1)
        shared = pull_sums(lhs, rhs, sums)
        for side, tile in enumerate(tiles):
            acc = accs[side] + shared[16 * side : 16 * side + 16]
            out_ref[:, pl.ds(pl.multiple_of(tile * TILE, TILE), TILE)] = acc[0:8] + acc[8:16]
        return carry

    lax.fori_loop(0, lhs_ref.shape[0] // 2, two_tiles, 0, unroll=UNROLL // 2)


def other_layer_kernel(
    names_ref, flags_ref, layer_ref, lhs_ref, below_ref, own_ref, above_ref,
    sums_ref, vel_ref, body_ref, react_ref, disp_out_ref, vel_out_ref, table_ref,
):
    layer = layer_ref[0]
    for side, ref, edge in ((0, below_ref, 0), (1, above_ref, 3)):

        @pl.when(layer == edge)
        def _():
            for sector in range(5):
                fill_table(own_ref, table_ref, sector * 8, sector * 2 + side, 512)

        @pl.when(layer != edge)
        def _():
            for sector in range(5):
                fill_table(ref, table_ref, sector * 8, sector * 2 + side, 512)

    def one_tile(tile, carry):
        lanes = pl.ds(pl.multiple_of(tile * TILE, TILE), TILE)
        word = flags_ref[tile // 2]
        acc = pair_sums(tile, other_slots, table_ref, names_ref, word, lhs_ref[tile])
        acc = acc[0:8] + acc[8:16] + sums_ref[:, lanes]
        own = own_ref[16:24, lanes]
        disp = own[3:6]
        now = own[0:3] + disp
        whole = 1.0 - own[6:7]
        inner = acc[0:3] - now * acc[6:7]
        outer = acc[3:6] - now * acc[7:8]
        force = force_scale * whole * (own[7:8] * inner + outer)
        force += react_ref[:, lanes]
        for c in range(3):
            load = force[c : c + 1] + body_ref[c, :, lanes]
            vel = vel_ref[c, :, lanes] + time_step * load
            vel_out_ref[c, :, lanes] = vel
            disp_out_ref[c, :, lanes] = disp[c : c + 1] + time_step * vel
        return carry

    lax.fori_loop(0, lhs_ref.shape[0], one_tile, 0, unroll=UNROLL_OTHER)


def cost(flops):
    return pl.CostEstimate(flops=flops, transcendentals=0, bytes_accessed=6_000_000)


smem = pl.BlockSpec(memory_space=pltpu.SMEM)
vmem = pl.BlockSpec(memory_space=pltpu.VMEM)


def own_layer_sums(names, flags, lhs, blocks):
    points = blocks[0].shape[1]
    return pl.pallas_call(
        own_layer_kernel,
        out_shape=jax.ShapeDtypeStruct((8, points), f32),
        in_specs=[smem, smem] + [vmem] * (1 + len(blocks)),
        out_specs=vmem,
        scratch_shapes=[pltpu.VMEM((len(blocks), 48, points), bf16)],
        name="own_layer",
        cost_estimate=cost(18_000_000_000),
    )(names, flags, lhs, *blocks)


def other_layer_update(names, flags, layer, lhs, below, own, above, sums, vel, body, react):
    points = own.shape[1]
    shape = jax.ShapeDtypeStruct((3, 1, points), f32)
    return pl.pallas_call(
        other_layer_kernel,
        out_shape=(shape, shape),
        in_specs=[smem] * 3 + [vmem] * 8,
        out_specs=(vmem, vmem),
        scratch_shapes=[pltpu.VMEM((10, 48, points), bf16)],
        name="other_layer",
        cost_estimate=cost(36_000_000_000),
    )(names, flags, layer, lhs, below, own, above, sums, vel, body, react)


def parts32(value):
    high, middle, low = split3(value)
    return jnp.concatenate([high, middle, low, jnp.zeros_like(low)], axis=0)


def parts16(value):
    row = lax.broadcasted_iota(jnp.int32, value.shape, 0)
    high, middle, low = split3(value)
    return jnp.concatenate([jnp.where(row < 3, pltpu.roll(middle, 5, 0), high), low], axis=0)


def join16(value):
    return value[3:6] + value[0:3] + value[11:14]


def join32(value):
    return value[0:8] + value[8:16] + value[16:24]


def one_hot(index, count):
    row = lax.broadcasted_iota(jnp.int32, (count, index.shape[1]), 0)
    return jnp.where(row == index, 1.0, 0.0).astype(bf16)


def slot_row(index_ref):
    return jnp.concatenate([index_ref[c : c + 1, :] for c in range(index_ref.shape[0])], axis=1)


def values_kernel(field_ref, blade_ref, rim_ref, root_ref, out_ref, pad_ref):
    rim = slot_row(rim_ref)
    root = slot_row(root_ref)
    tile_of = lax.shift_right_logical(rim, 7)
    lane_hot = one_hot(rim & 127, TILE)

    def one_batch(step, acc):
        rows = []
        for inner in range(8):
            start = pl.multiple_of(step * (8 * TILE) + inner * TILE, TILE)
            rows.append(parts16(field_ref[:, pl.ds(start, TILE)]))
        found = jnp.dot(jnp.concatenate(rows, axis=0).astype(bf16), lane_hot, preferred_element_type=f32)
        for inner in range(8):
            acc = acc + jnp.where(tile_of == step * 8 + inner, found[inner * 16 : inner * 16 + 16], 0.0)
        return acc

    acc = lax.fori_loop(0, field_ref.shape[1] // (8 * TILE), one_batch, jnp.zeros((16, rim.shape[1]), f32))
    out_ref[0:3] = join16(acc)
    pad_ref[...] = jnp.zeros_like(pad_ref)
    for c in range(3):
        pad_ref[c : c + 1] = blade_ref[c]
    found = jnp.dot(
        parts32(pad_ref[...]).astype(bf16), one_hot(root, blade_ref.shape[2]), preferred_element_type=f32
    )
    out_ref[3:6] = join32(found)[0:3]


def coupling_values(field, blade, rim, root):
    return pl.pallas_call(
        values_kernel,
        out_shape=jax.ShapeDtypeStruct((6, rim.shape[0] * rim.shape[1]), f32),
        scratch_shapes=[pltpu.VMEM((8, blade.shape[2]), f32)],
        name="coupling_values",
        cost_estimate=cost(3_000_000_000),
    )(field, blade, rim, root)


def coupling_kernel(
    swapped_ref, sent_ref, rim_ref, root_ref, nodes_ref, scale_ref, stiff_ref, blade_ref, vel_ref,
    after_ref, react_ref, disp_out_ref, vel_out_ref, pad_ref, elem_ref,
):
    nodes = blade_ref.shape[2]
    rim = slot_row(rim_ref)
    root = slot_row(root_ref)
    tile_of = lax.shift_right_logical(rim, 7)
    lane_hot = one_hot(rim & 127, TILE)
    pad_ref[...] = jnp.zeros_like(pad_ref)
    pad_ref[3:6] = spring * (swapped_ref[3:6] - sent_ref[0:3])
    back = parts16(pad_ref[...])
    pad_ref[...] = jnp.zeros_like(pad_ref)

    def one_batch(step, carry):
        rows = jnp.concatenate(
            [jnp.where(tile_of == step * 8 + inner, back, 0.0) for inner in range(8)], axis=0
        )
        put = lax.dot_general(rows.astype(bf16), lane_hot, across, preferred_element_type=f32)
        for inner in range(8):
            start = pl.multiple_of(step * (8 * TILE) + inner * TILE, TILE)
            react_ref[:, pl.ds(start, TILE)] = join16(put[inner * 16 : inner * 16 + 16])
        return carry

    lax.fori_loop(0, react_ref.shape[1] // (8 * TILE), one_batch, 0)
    pad_ref[0:3] = spring * (swapped_ref[0:3] - sent_ref[3:6])
    loads = parts32(pad_ref[...]).astype(bf16)
    coupling = join32(
        lax.dot_general(loads, one_hot(root, nodes), across, preferred_element_type=f32)
    )
    for c in range(3):
        pad_ref[c : c + 1] = blade_ref[c]
    blade = parts32(pad_ref[...]).astype(bf16)
    hots = []
    for q in range(8):
        hot = one_hot(nodes_ref[q : q + 1], nodes)
        hots.append(hot)
        taken = join32(jnp.dot(blade, hot, preferred_element_type=f32))
        for a in range(3):
            elem_ref[8 * a + q : 8 * a + q + 1, :] = taken[a : a + 1]
    force = scale_ref[...] * jnp.dot(
        stiff_ref[...], elem_ref[...], precision=lax.Precision.HIGHEST, preferred_element_type=f32
    )
    high, middle, low = split3(force)
    force = jnp.concatenate([high, middle, low, jnp.zeros((8, force.shape[1]), f32)], axis=0).astype(bf16)
    row = lax.broadcasted_iota(jnp.int32, (24, nodes), 0)
    total = jnp.zeros((24, nodes), f32)
    for q in range(8):
        put = lax.dot_general(force, hots[q], across, preferred_element_type=f32)
        total = total + jnp.where(row % 8 == q, put[0:24] + put[24:48] + put[48:72], 0.0)
    for a in range(3):
        internal = -jnp.sum(total[8 * a : 8 * a + 8], axis=0, keepdims=True)
        vel = vel_ref[a] + time_step * (internal + coupling[a : a + 1])
        vel_out_ref[a] = vel
        disp_out_ref[a] = blade_ref[a] + time_step * vel


def coupling_update(swapped, sent, rim, root, nodes, scale, stiff, blade, vel, after, points):
    small = jax.ShapeDtypeStruct(blade.shape, f32)
    return pl.pallas_call(
        coupling_kernel,
        out_shape=(jax.ShapeDtypeStruct((3, points), f32), small, small),
        scratch_shapes=[
            pltpu.VMEM((8, blade.shape[2]), f32),
            pltpu.VMEM((24, nodes.shape[1]), f32),
        ],
        in_specs=[vmem] * 9 + [pl.BlockSpec(memory_space=pl.ANY)],
        name="coupling_update",
        cost_estimate=cost(4_000_000_000),
    )(swapped, sent, rim, root, nodes, scale, stiff, blade, vel, after)


def shift_layer(value, by):
    size = lax.axis_size("layer")
    pairs = [(i, i + by) for i in range(size) if 0 <= i + by < size]
    return lax.ppermute(value, "layer", pairs)


def shift_sector(value, by):
    size = lax.axis_size("blk")
    return lax.ppermute(value, "blk", [(i, (i + by) % size) for i in range(size)])


def on_device(
    ref_pos,
    disk_disp,
    disk_vel,
    damage,
    modulus,
    body_load,
    nbr_tiles,
    break_flags,
    blade_disp,
    blade_vel,
    elem_nodes,
    elem_modulus,
    elem_stiff,
    root_nodes,
    rim_points,
):
    disk_now = disk_disp[0, 0]
    field = jnp.concatenate([ref_pos[0, 0], disk_now, damage[0], modulus[0]], axis=0)
    names = nbr_tiles[0, 0].T
    flags = break_flags[0, 0]
    far_behind = shift_sector(field, 2)
    behind = shift_sector(field, 1)
    rim = rim_points[0, 0].T
    root = root_nodes[0, 0].T
    blade_rows = blade_disp.reshape(3, 1, -1)
    sent = coupling_values(field, blade_rows, rim, root)
    later, sent = lax.optimization_barrier((field, sent))
    ahead = shift_sector(later, -1)
    far_ahead = shift_sector(later, -2)
    swapped = lax.all_to_all(
        sent.reshape(6, rim.shape[0], rim.shape[1]), "blk", split_axis=2, concat_axis=2, tiled=True
    )
    lhs = own_table(field)
    blocks = [far_behind, behind, field, ahead, far_ahead]
    own = jnp.concatenate(blocks, axis=0)
    below = shift_layer(own, 1)
    above = shift_layer(own, -1)
    sums = own_layer_sums(names, flags, lhs, blocks)
    swapped, sums = lax.optimization_barrier((swapped, sums))
    swapped = swapped.reshape(sent.shape)
    reaction, blade_disp_new, blade_vel_new = coupling_update(
        swapped, sent, rim, root, elem_nodes[0, 0], elem_modulus[0], elem_stiff, blade_rows,
        blade_vel.reshape(3, 1, -1), sums, field.shape[1],
    )
    layer = lax.axis_index("layer").reshape(1).astype(jnp.int32)
    disk_disp_new, disk_vel_new = other_layer_update(
        names, flags, layer, lhs, below, own, above, sums, disk_vel.reshape(3, 1, -1),
        body_load.reshape(3, 1, -1), reaction
    )
    return (
        disk_disp_new.reshape(disk_disp.shape),
        disk_vel_new.reshape(disk_vel.shape),
        blade_disp_new.reshape(blade_disp.shape),
        blade_vel_new.reshape(blade_vel.shape),
    )


def solution(mesh):
    in_specs = (
        P("blk", "layer", None, None),
        P("blk", "layer", None, None),
        P("blk", "layer", None, None),
        P("blk", "layer", None),
        P("blk", "layer", None),
        P("blk", "layer", None, None),
        P("blk", "layer", None, None),
        P("blk", "layer", None),
        P("blk", "layer", None, None),
        P("blk", "layer", None, None),
        P("blk", "layer", None, None),
        P("blk", "layer", None),
        P(),
        P("blk", "layer", None, None),
        P("blk", "layer", None, None),
    )
    out_specs = (
        P("blk", "layer", None, None),
        P("blk", "layer", None, None),
        P("blk", "layer", None, None),
        P("blk", "layer", None, None),
    )
    return jax.shard_map(
        on_device, mesh=mesh, in_specs=in_specs, out_specs=out_specs, check_vma=False
    )
```

```python
import math
import jax
import jax.numpy as jnp
from jax import lax
from jax.experimental import pallas as pl
from jax.experimental.pallas import tpu as pltpu
from jax.sharding import PartitionSpec as P

TILE = 128
log_scale = math.log2(math.e) / 9.0
force_scale = -0.125 * log_scale * math.exp(1.0 / 9.0)
f32 = jnp.float32
across = (((1,), (1,)), ((), ()))
bf16 = jnp.bfloat16
UNROLL = 16
UNROLL_OTHER = 8
own_slots = (1, 4, 7, 10, 13)
other_slots = (0, 2, 3, 5, 6, 8, 9, 11, 12, 14)
OWN_UNROLL = 8
spring = 0.5
time_step = 0.5


def split3(value):
    high = value.astype(bf16).astype(f32)
    rest = value - high
    middle = rest.astype(bf16).astype(f32)
    return high, middle, (rest - middle)


def point_terms(v):
    row = lax.broadcasted_iota(jnp.int32, v.shape, 0)
    disp = pltpu.roll(v, 5, 0)
    now = v + disp
    first = row < 3
    ref_norm = jnp.sum(jnp.where(first, v * v, 0.0), axis=0, keepdims=True)
    growth = jnp.sum(jnp.where(first, disp * (v + now), 0.0), axis=0, keepdims=True)
    return row, disp, now, ref_norm, growth


def own_kernel(field_ref, lhs_ref):
    def one_tile(tile, carry):
        v = field_ref[:, pl.ds(pl.multiple_of(tile * TILE, TILE), TILE)]
        row, disp, now, ref_norm, growth = point_terms(v)
        row16 = lax.broadcasted_iota(jnp.int32, (16, TILE), 0)
        coef_ref = jnp.where(row < 3, 2.0 * log_scale * v, jnp.where(row == 6, -log_scale, 0.0))
        coef_now = jnp.where(
            row < 3,
            -2.0 * disp,
            jnp.where(row < 6, -2.0 * pltpu.roll(now, 3, 0), jnp.where(row == 7, 1.0, 0.0)),
        )
        for place, coef, alone in (
            (0, coef_ref, -log_scale * (1.0 + ref_norm)),
            (1, coef_now, growth),
        ):
            high, middle, low = split3(coef)
            a, b, c = split3(alone)
            const = jnp.where(row16 == 0, a, jnp.where(row16 == 1, b, jnp.where(row16 == 2, c, 0.0)))
            rows = jnp.concatenate([high, high, middle, middle, high, low, const], axis=0)
            lhs_ref[tile, pl.ds(place * TILE, TILE), :] = rows.T.astype(bf16)
        return carry

    lax.fori_loop(0, field_ref.shape[1] // TILE, one_tile, 0, unroll=OWN_UNROLL)


def own_table(field):
    tiles = field.shape[1] // TILE
    return pl.pallas_call(
        own_kernel,
        out_shape=jax.ShapeDtypeStruct((tiles, 2 * TILE, 64), bf16),
        name="own_table",
        cost_estimate=pl.CostEstimate(flops=8_000_000_000, transcendentals=0, bytes_accessed=4_500_000),
    )(field)


def fill_table(field_ref, table_ref, row_start, place, chunk):
    def one(step, carry):
        lanes = pl.ds(pl.multiple_of(step * chunk, chunk), chunk)
        v = field_ref[row_start : row_start + 8, lanes]
        row = lax.broadcasted_iota(jnp.int32, v.shape, 0)
        now = v + pltpu.roll(v, 5, 0)
        grown = v * (v + jnp.where(row < 3, 0.0, 2.0 * pltpu.roll(v, 3, 0)))
        summed = grown + pltpu.roll(grown, 7, 0) + pltpu.roll(grown, 6, 0)
        terms = jnp.where(row < 6, v, jnp.where(row == 6, pltpu.roll(summed, 6, 0), pltpu.roll(summed, 4, 0)))
        high, middle, low = split3(terms)
        table_ref[place, 0:16, lanes] = jnp.concatenate([high, middle], axis=0).astype(bf16)
        table_ref[place, 16:32, lanes] = jnp.concatenate([low, high], axis=0).astype(bf16)
        whole = 1.0 - v[6:7]
        stiff = v[7:8]
        spread = jnp.where(row < 3, now, jnp.where(row < 6, pltpu.roll(now, 3, 0), 1.0))
        weight = whole * jnp.where((row < 3) | (row == 6), 1.0, stiff)
        sums = spread * weight
        q_high = sums.astype(bf16).astype(f32)
        table_ref[place, 32:48, lanes] = jnp.concatenate([q_high, sums - q_high], axis=0).astype(bf16)
        return carry

    lax.fori_loop(0, field_ref.shape[1] // chunk, one, 0)


def slot_terms(tile, slot, place, table_ref, names_ref, word):
    name = names_ref[slot, tile]
    lanes = pl.ds(pl.multiple_of((name % 64) * TILE, TILE), TILE)
    top = table_ref[place, 0:16, lanes]
    low = table_ref[place, 16:32, lanes]
    alive = 1 - (lax.shift_right_logical(word, (tile % 2) * 15 + slot) & 1)
    q = table_ref[place, 32:48, lanes]
    rhs = jnp.concatenate([top, top, low, jnp.ones((16, TILE), bf16)], axis=0)
    return rhs, jnp.where(alive == 1, q, jnp.zeros_like(q))


def pull_sums(lhs, rhs, sums):
    both = jnp.dot(lhs, rhs, preferred_element_type=f32)
    stretch = both[:TILE]
    pull = both[TILE:] * jnp.exp2(stretch) / stretch
    high = pull.astype(bf16)
    low = (pull - high.astype(f32)).astype(bf16)
    part = lax.dot_general(sums, high, across, preferred_element_type=f32)
    return part + lax.dot_general(sums, low, across, preferred_element_type=f32)


def pair_sums(tile, slots, table_ref, names_ref, word, lhs):
    acc = None
    for start in range(0, len(slots), 2):
        terms = [
            slot_terms(tile, slots[place], place, table_ref, names_ref, word) for place in (start, start + 1)
        ]
        part = pull_sums(
            lhs,
            jnp.concatenate([terms[0][0], terms[1][0]], axis=1),
            jnp.concatenate([terms[0][1], terms[1][1]], axis=1),
        )
        acc = part if acc is None else acc + part
    return acc


def own_layer_kernel(names_ref, flags_ref, lhs_ref, *refs):
    out_ref, table_ref = refs[-2:]
    for place, ref in enumerate(refs[:-2]):
        fill_table(ref, table_ref, 0, place, 512)

    last = len(own_slots) - 1

    def two_tiles(pair, carry):
        word = flags_ref[pair]
        tiles = (2 * pair, 2 * pair + 1)
        accs = [
            pair_sums(tile, own_slots[:last], table_ref, names_ref, word, lhs_ref[tile]) for tile in tiles
        ]
        terms = [slot_terms(tile, own_slots[last], last, table_ref, names_ref, word) for tile in tiles]
        none_rhs, none_sums = (jnp.zeros_like(part) for part in terms[0])
        rhs = jnp.concatenate(
            [
                jnp.concatenate([terms[0][0], none_rhs], axis=1),
                jnp.concatenate([none_rhs, terms[1][0]], axis=1),
            ],
            axis=0,
        )
        sums = jnp.concatenate(
            [
                jnp.concatenate([terms[0][1], none_sums], axis=1),
                jnp.concatenate([none_sums, terms[1][1]], axis=1),
            ],
            axis=0,
        )
        lhs = jnp.concatenate([lhs_ref[tiles[0]], lhs_ref[tiles[1]]], axis=1)
        shared = pull_sums(lhs, rhs, sums)
        for side, tile in enumerate(tiles):
            acc = accs[side] + shared[16 * side : 16 * side + 16]
            out_ref[:, pl.ds(pl.multiple_of(tile * TILE, TILE), TILE)] = acc[0:8] + acc[8:16]
        return carry

    lax.fori_loop(0, lhs_ref.shape[0] // 2, two_tiles, 0, unroll=UNROLL // 2)


def other_layer_kernel(
    names_ref, flags_ref, layer_ref, lhs_ref, below_ref, own_ref, above_ref,
    sums_ref, vel_ref, body_ref, react_ref, disp_out_ref, vel_out_ref, table_ref,
):
    layer = layer_ref[0]
    for side, ref, edge in ((0, below_ref, 0), (1, above_ref, 3)):

        @pl.when(layer == edge)
        def _():
            for sector in range(5):
                fill_table(own_ref, table_ref, sector * 8, sector * 2 + side, 512)

        @pl.when(layer != edge)
        def _():
            for sector in range(5):
                fill_table(ref, table_ref, sector * 8, sector * 2 + side, 512)

    def one_tile(tile, carry):
        lanes = pl.ds(pl.multiple_of(tile * TILE, TILE), TILE)
        word = flags_ref[tile // 2]
        acc = pair_sums(tile, other_slots, table_ref, names_ref, word, lhs_ref[tile])
        acc = acc[0:8] + acc[8:16] + sums_ref[:, lanes]
        own = own_ref[16:24, lanes]
        disp = own[3:6]
        now = own[0:3] + disp
        whole = 1.0 - own[6:7]
        inner = acc[0:3] - now * acc[6:7]
        outer = acc[3:6] - now * acc[7:8]
        force = force_scale * whole * (own[7:8] * inner + outer)
        force += react_ref[:, lanes]
        for c in range(3):
            load = force[c : c + 1] + body_ref[c, :, lanes]
            vel = vel_ref[c, :, lanes] + time_step * load
            vel_out_ref[c, :, lanes] = vel
            disp_out_ref[c, :, lanes] = disp[c : c + 1] + time_step * vel
        return carry

    lax.fori_loop(0, lhs_ref.shape[0], one_tile, 0, unroll=UNROLL_OTHER)


def cost(flops):
    return pl.CostEstimate(flops=flops, transcendentals=0, bytes_accessed=6_000_000)


smem = pl.BlockSpec(memory_space=pltpu.SMEM)
vmem = pl.BlockSpec(memory_space=pltpu.VMEM)


def own_layer_sums(names, flags, lhs, blocks):
    points = blocks[0].shape[1]
    return pl.pallas_call(
        own_layer_kernel,
        out_shape=jax.ShapeDtypeStruct((8, points), f32),
        in_specs=[smem, smem] + [vmem] * (1 + len(blocks)),
        out_specs=vmem,
        scratch_shapes=[pltpu.VMEM((len(blocks), 48, points), bf16)],
        name="own_layer",
        cost_estimate=cost(18_000_000_000),
    )(names, flags, lhs, *blocks)


def other_layer_update(names, flags, layer, lhs, below, own, above, sums, vel, body, react):
    points = own.shape[1]
    shape = jax.ShapeDtypeStruct((3, 1, points), f32)
    return pl.pallas_call(
        other_layer_kernel,
        out_shape=(shape, shape),
        in_specs=[smem] * 3 + [vmem] * 8,
        out_specs=(vmem, vmem),
        scratch_shapes=[pltpu.VMEM((10, 48, points), bf16)],
        name="other_layer",
        cost_estimate=cost(36_000_000_000),
    )(names, flags, layer, lhs, below, own, above, sums, vel, body, react)


def parts32(value):
    high, middle, low = split3(value)
    return jnp.concatenate([high, middle, low, jnp.zeros_like(low)], axis=0)


def parts16(value):
    row = lax.broadcasted_iota(jnp.int32, value.shape, 0)
    high, middle, low = split3(value)
    return jnp.concatenate([jnp.where(row < 3, pltpu.roll(middle, 5, 0), high), low], axis=0)


def join16(value):
    return value[3:6] + value[0:3] + value[11:14]


def join32(value):
    return value[0:8] + value[8:16] + value[16:24]


def one_hot(index, count):
    row = lax.broadcasted_iota(jnp.int32, (count, index.shape[1]), 0)
    return jnp.where(row == index, 1.0, 0.0).astype(bf16)


def slot_row(index_ref):
    return jnp.concatenate([index_ref[c : c + 1, :] for c in range(index_ref.shape[0])], axis=1)


def values_kernel(
    pos_ref, disp_ref, damage_ref, modulus_ref, blade_ref, rim_ref, root_ref, field_ref, out_ref, pad_ref
):
    for c in range(3):
        field_ref[c : c + 1, :] = pos_ref[c]
        field_ref[3 + c : 4 + c, :] = disp_ref[c]
    field_ref[6:7, :] = damage_ref[...]
    field_ref[7:8, :] = modulus_ref[...]
    rim = slot_row(rim_ref)
    root = slot_row(root_ref)
    tile_of = lax.shift_right_logical(rim, 7)
    lane_hot = one_hot(rim & 127, TILE)

    def one_batch(step, acc):
        rows = []
        for inner in range(8):
            start = pl.multiple_of(step * (8 * TILE) + inner * TILE, TILE)
            rows.append(parts16(field_ref[:, pl.ds(start, TILE)]))
        found = jnp.dot(jnp.concatenate(rows, axis=0).astype(bf16), lane_hot, preferred_element_type=f32)
        for inner in range(8):
            acc = acc + jnp.where(tile_of == step * 8 + inner, found[inner * 16 : inner * 16 + 16], 0.0)
        return acc

    acc = lax.fori_loop(0, field_ref.shape[1] // (8 * TILE), one_batch, jnp.zeros((16, rim.shape[1]), f32))
    at_rim = join16(acc)
    pad_ref[...] = jnp.zeros_like(pad_ref)
    for c in range(3):
        pad_ref[c : c + 1] = blade_ref[c]
    found = jnp.dot(
        parts32(pad_ref[...]).astype(bf16), one_hot(root, blade_ref.shape[2]), preferred_element_type=f32
    )
    values = jnp.concatenate([at_rim, join32(found)[0:3]], axis=0)
    width = rim_ref.shape[1]
    for c in range(rim_ref.shape[0]):
        out_ref[:, c, :] = values[:, c * width : (c + 1) * width]


def coupling_values(pos, disp, damage, modulus, blade, rim, root):
    return pl.pallas_call(
        values_kernel,
        out_shape=(
            jax.ShapeDtypeStruct((8, pos.shape[2]), f32),
            jax.ShapeDtypeStruct((6, *rim.shape), f32),
        ),
        scratch_shapes=[pltpu.VMEM((8, blade.shape[2]), f32)],
        name="coupling_values",
        cost_estimate=cost(3_000_000_000),
    )(pos, disp, damage, modulus, blade, rim, root)


def slot_values(values_ref):
    return jnp.concatenate([values_ref[:, c, :] for c in range(values_ref.shape[1])], axis=1)


def coupling_kernel(
    swapped_ref, sent_ref, rim_ref, root_ref, nodes_ref, scale_ref, stiff_ref, blade_ref, vel_ref,
    after_ref, react_ref, disp_out_ref, vel_out_ref, pad_ref, elem_ref,
):
    nodes = blade_ref.shape[2]
    rim = slot_row(rim_ref)
    root = slot_row(root_ref)
    tile_of = lax.shift_right_logical(rim, 7)
    lane_hot = one_hot(rim & 127, TILE)
    pad_ref[...] = jnp.zeros_like(pad_ref)
    swapped = slot_values(swapped_ref)
    sent = slot_values(sent_ref)
    pad_ref[3:6] = spring * (swapped[3:6] - sent[0:3])
    back = parts16(pad_ref[...])
    pad_ref[...] = jnp.zeros_like(pad_ref)

    def one_batch(step, carry):
        rows = jnp.concatenate(
            [jnp.where(tile_of == step * 8 + inner, back, 0.0) for inner in range(8)], axis=0
        )
        put = lax.dot_general(rows.astype(bf16), lane_hot, across, preferred_element_type=f32)
        for inner in range(8):
            start = pl.multiple_of(step * (8 * TILE) + inner * TILE, TILE)
            react_ref[:, pl.ds(start, TILE)] = join16(put[inner * 16 : inner * 16 + 16])
        return carry

    lax.fori_loop(0, react_ref.shape[1] // (8 * TILE), one_batch, 0)
    pad_ref[0:3] = spring * (swapped[0:3] - sent[3:6])
    loads = parts32(pad_ref[...]).astype(bf16)
    coupling = join32(
        lax.dot_general(loads, one_hot(root, nodes), across, preferred_element_type=f32)
    )
    for c in range(3):
        pad_ref[c : c + 1] = blade_ref[c]
    blade = parts32(pad_ref[...]).astype(bf16)
    hots = []
    for q in range(8):
        hot = one_hot(nodes_ref[q : q + 1], nodes)
        hots.append(hot)
        taken = join32(jnp.dot(blade, hot, preferred_element_type=f32))
        for a in range(3):
            elem_ref[8 * a + q : 8 * a + q + 1, :] = taken[a : a + 1]
    force = scale_ref[...] * jnp.dot(
        stiff_ref[...], elem_ref[...], precision=lax.Precision.HIGHEST, preferred_element_type=f32
    )
    high, middle, low = split3(force)
    force = jnp.concatenate([high, middle, low, jnp.zeros((8, force.shape[1]), f32)], axis=0).astype(bf16)
    row = lax.broadcasted_iota(jnp.int32, (24, nodes), 0)
    total = jnp.zeros((24, nodes), f32)
    for q in range(8):
        put = lax.dot_general(force, hots[q], across, preferred_element_type=f32)
        total = total + jnp.where(row % 8 == q, put[0:24] + put[24:48] + put[48:72], 0.0)
    for a in range(3):
        internal = -jnp.sum(total[8 * a : 8 * a + 8], axis=0, keepdims=True)
        vel = vel_ref[a] + time_step * (internal + coupling[a : a + 1])
        vel_out_ref[a] = vel
        disp_out_ref[a] = blade_ref[a] + time_step * vel


def coupling_update(swapped, sent, rim, root, nodes, scale, stiff, blade, vel, after, points):
    small = jax.ShapeDtypeStruct(blade.shape, f32)
    return pl.pallas_call(
        coupling_kernel,
        out_shape=(jax.ShapeDtypeStruct((3, points), f32), small, small),
        scratch_shapes=[
            pltpu.VMEM((8, blade.shape[2]), f32),
            pltpu.VMEM((24, nodes.shape[1]), f32),
        ],
        in_specs=[vmem] * 9 + [pl.BlockSpec(memory_space=pl.ANY)],
        name="coupling_update",
        cost_estimate=cost(4_000_000_000),
    )(swapped, sent, rim, root, nodes, scale, stiff, blade, vel, after)


def stack_kernel(*refs):
    out_ref, sems = refs[-2:]
    copies = []
    for place, ref in enumerate(refs[:-2]):
        copies.append(pltpu.make_async_copy(ref, out_ref.at[pl.ds(8 * place, 8), :], sems.at[place]))
    for copy in copies:
        copy.start()
    for copy in copies:
        copy.wait()


def stacked(blocks):
    raw = pl.BlockSpec(memory_space=pl.ANY)
    return pl.pallas_call(
        stack_kernel,
        out_shape=jax.ShapeDtypeStruct((8 * len(blocks), blocks[0].shape[1]), f32),
        in_specs=[raw] * len(blocks),
        out_specs=raw,
        scratch_shapes=[pltpu.SemaphoreType.DMA((len(blocks),))],
        name="stacked",
    )(*blocks)


def shift_layer(value, by):
    size = lax.axis_size("layer")
    pairs = [(i, i + by) for i in range(size) if 0 <= i + by < size]
    return lax.ppermute(value, "layer", pairs)


def shift_sector(value, by):
    size = lax.axis_size("blk")
    return lax.ppermute(value, "blk", [(i, (i + by) % size) for i in range(size)])


def on_device(
    ref_pos,
    disk_disp,
    disk_vel,
    damage,
    modulus,
    body_load,
    nbr_tiles,
    break_flags,
    blade_disp,
    blade_vel,
    elem_nodes,
    elem_modulus,
    elem_stiff,
    root_nodes,
    rim_points,
):
    names = nbr_tiles[0, 0].T
    flags = break_flags[0, 0]
    rim = rim_points[0, 0].T
    root = root_nodes[0, 0].T
    blade_rows = blade_disp.reshape(3, 1, -1)
    field, sent = coupling_values(
        ref_pos.reshape(3, 1, -1), disk_disp.reshape(3, 1, -1), damage[0], modulus[0], blade_rows, rim, root
    )
    ahead = shift_sector(field, -1)
    far_ahead = shift_sector(field, -2)
    far_behind = shift_sector(field, 2)
    behind = shift_sector(field, 1)
    swapped = lax.all_to_all(sent, "blk", split_axis=2, concat_axis=2, tiled=True)
    lhs = own_table(field)
    blocks = [far_behind, behind, field, ahead, far_ahead]
    own = stacked(blocks)
    below = shift_layer(own, 1)
    above = shift_layer(own, -1)
    sums = own_layer_sums(names, flags, lhs, blocks)
    swapped, sums = lax.optimization_barrier((swapped, sums))
    reaction, blade_disp_new, blade_vel_new = coupling_update(
        swapped, sent, rim, root, elem_nodes[0, 0], elem_modulus[0], elem_stiff, blade_rows,
        blade_vel.reshape(3, 1, -1), sums, field.shape[1],
    )
    layer = lax.axis_index("layer").reshape(1).astype(jnp.int32)
    disk_disp_new, disk_vel_new = other_layer_update(
        names, flags, layer, lhs, below, own, above, sums, disk_vel.reshape(3, 1, -1),
        body_load.reshape(3, 1, -1), reaction
    )
    return (
        disk_disp_new.reshape(disk_disp.shape),
        disk_vel_new.reshape(disk_vel.shape),
        blade_disp_new.reshape(blade_disp.shape),
        blade_vel_new.reshape(blade_vel.shape),
    )


def solution(mesh):
    in_specs = (
        P("blk", "layer", None, None),
        P("blk", "layer", None, None),
        P("blk", "layer", None, None),
        P("blk", "layer", None),
        P("blk", "layer", None),
        P("blk", "layer", None, None),
        P("blk", "layer", None, None),
        P("blk", "layer", None),
        P("blk", "layer", None, None),
        P("blk", "layer", None, None),
        P("blk", "layer", None, None),
        P("blk", "layer", None),
        P(),
        P("blk", "layer", None, None),
        P("blk", "layer", None, None),
    )
    out_specs = (
        P("blk", "layer", None, None),
        P("blk", "layer", None, None),
        P("blk", "layer", None, None),
        P("blk", "layer", None, None),
    )
    return jax.shard_map(
        on_device, mesh=mesh, in_specs=in_specs, out_specs=out_specs, check_vma=False
    )
```

```python
import math
import jax
import jax.numpy as jnp
from jax import lax
from jax.experimental import pallas as pl
from jax.experimental.pallas import tpu as pltpu
from jax.sharding import PartitionSpec as P

TILE = 128
log_scale = math.log2(math.e) / 9.0
force_scale = -0.125 * log_scale * math.exp(1.0 / 9.0)
f32 = jnp.float32
across = (((1,), (1,)), ((), ()))
bf16 = jnp.bfloat16
UNROLL = 16
UNROLL_OTHER = 8
own_slots = (1, 4, 7, 10, 13)
other_slots = (0, 2, 3, 5, 6, 8, 9, 11, 12, 14)
OWN_UNROLL = 8
spring = 0.5
time_step = 0.5


def split3(value):
    high = value.astype(bf16).astype(f32)
    rest = value - high
    middle = rest.astype(bf16).astype(f32)
    return high, middle, (rest - middle)


def point_terms(v):
    row = lax.broadcasted_iota(jnp.int32, v.shape, 0)
    disp = pltpu.roll(v, 5, 0)
    now = v + disp
    first = row < 3
    ref_norm = jnp.sum(jnp.where(first, v * v, 0.0), axis=0, keepdims=True)
    growth = jnp.sum(jnp.where(first, disp * (v + now), 0.0), axis=0, keepdims=True)
    return row, disp, now, ref_norm, growth


def own_kernel(field_ref, lhs_ref):
    def one_tile(tile, carry):
        v = field_ref[:, pl.ds(pl.multiple_of(tile * TILE, TILE), TILE)]
        row, disp, now, ref_norm, growth = point_terms(v)
        row16 = lax.broadcasted_iota(jnp.int32, (16, TILE), 0)
        coef_ref = jnp.where(row < 3, 2.0 * log_scale * v, jnp.where(row == 6, -log_scale, 0.0))
        coef_now = jnp.where(
            row < 3,
            -2.0 * disp,
            jnp.where(row < 6, -2.0 * pltpu.roll(now, 3, 0), jnp.where(row == 7, 1.0, 0.0)),
        )
        for place, coef, alone in (
            (0, coef_ref, -log_scale * (1.0 + ref_norm)),
            (1, coef_now, growth),
        ):
            high, middle, low = split3(coef)
            a, b, c = split3(alone)
            const = jnp.where(row16 == 0, a, jnp.where(row16 == 1, b, jnp.where(row16 == 2, c, 0.0)))
            rows = jnp.concatenate([high, high, middle, middle, high, low, const], axis=0)
            lhs_ref[tile, pl.ds(place * TILE, TILE), :] = rows.T.astype(bf16)
        return carry

    lax.fori_loop(0, field_ref.shape[1] // TILE, one_tile, 0, unroll=OWN_UNROLL)


def own_table(field):
    tiles = field.shape[1] // TILE
    return pl.pallas_call(
        own_kernel,
        out_shape=jax.ShapeDtypeStruct((tiles, 2 * TILE, 64), bf16),
        name="own_table",
        cost_estimate=pl.CostEstimate(flops=8_000_000_000, transcendentals=0, bytes_accessed=4_500_000),
    )(field)


def fill_table(field_ref, table_ref, row_start, place, chunk):
    def one(step, carry):
        lanes = pl.ds(pl.multiple_of(step * chunk, chunk), chunk)
        v = field_ref[row_start : row_start + 8, lanes]
        row = lax.broadcasted_iota(jnp.int32, v.shape, 0)
        now = v + pltpu.roll(v, 5, 0)
        grown = v * (v + jnp.where(row < 3, 0.0, 2.0 * pltpu.roll(v, 3, 0)))
        summed = grown + pltpu.roll(grown, 7, 0) + pltpu.roll(grown, 6, 0)
        terms = jnp.where(row < 6, v, jnp.where(row == 6, pltpu.roll(summed, 6, 0), pltpu.roll(summed, 4, 0)))
        high, middle, low = split3(terms)
        table_ref[place, 0:16, lanes] = jnp.concatenate([high, middle], axis=0).astype(bf16)
        table_ref[place, 16:32, lanes] = jnp.concatenate([low, high], axis=0).astype(bf16)
        whole = 1.0 - v[6:7]
        stiff = v[7:8]
        spread = jnp.where(row < 3, now, jnp.where(row < 6, pltpu.roll(now, 3, 0), 1.0))
        weight = whole * jnp.where((row < 3) | (row == 6), 1.0, stiff)
        sums = spread * weight
        q_high = sums.astype(bf16).astype(f32)
        table_ref[place, 32:48, lanes] = jnp.concatenate([q_high, sums - q_high], axis=0).astype(bf16)
        return carry

    lax.fori_loop(0, field_ref.shape[1] // chunk, one, 0)


def slot_terms(tile, slot, place, table_ref, names_ref, word):
    name = names_ref[slot, tile]
    lanes = pl.ds(pl.multiple_of((name % 64) * TILE, TILE), TILE)
    top = table_ref[place, 0:16, lanes]
    low = table_ref[place, 16:32, lanes]
    alive = 1 - (lax.shift_right_logical(word, (tile % 2) * 15 + slot) & 1)
    q = table_ref[place, 32:48, lanes]
    rhs = jnp.concatenate([top, top, low, jnp.ones((16, TILE), bf16)], axis=0)
    return rhs, jnp.where(alive == 1, q, jnp.zeros_like(q))


def pull_sums(lhs, rhs, sums):
    both = jnp.dot(lhs, rhs, preferred_element_type=f32)
    stretch = both[:TILE]
    pull = both[TILE:] * jnp.exp2(stretch) / stretch
    high = pull.astype(bf16)
    low = (pull - high.astype(f32)).astype(bf16)
    part = lax.dot_general(sums, high, across, preferred_element_type=f32)
    return part + lax.dot_general(sums, low, across, preferred_element_type=f32)


def pair_sums(tile, slots, table_ref, names_ref, word, lhs):
    acc = None
    for start in range(0, len(slots), 2):
        terms = [
            slot_terms(tile, slots[place], place, table_ref, names_ref, word) for place in (start, start + 1)
        ]
        part = pull_sums(
            lhs,
            jnp.concatenate([terms[0][0], terms[1][0]], axis=1),
            jnp.concatenate([terms[0][1], terms[1][1]], axis=1),
        )
        acc = part if acc is None else acc + part
    return acc


def own_layer_kernel(names_ref, flags_ref, lhs_ref, *refs):
    out_ref, table_ref = refs[-2:]
    for place, ref in enumerate(refs[:-2]):
        fill_table(ref, table_ref, 0, place, 512)

    last = len(own_slots) - 1

    def two_tiles(pair, carry):
        word = flags_ref[pair]
        tiles = (2 * pair, 2 * pair + 1)
        accs = [
            pair_sums(tile, own_slots[:last], table_ref, names_ref, word, lhs_ref[tile]) for tile in tiles
        ]
        terms = [slot_terms(tile, own_slots[last], last, table_ref, names_ref, word) for tile in tiles]
        none_rhs, none_sums = (jnp.zeros_like(part) for part in terms[0])
        rhs = jnp.concatenate(
            [
                jnp.concatenate([terms[0][0], none_rhs], axis=1),
                jnp.concatenate([none_rhs, terms[1][0]], axis=1),
            ],
            axis=0,
        )
        sums = jnp.concatenate(
            [
                jnp.concatenate([terms[0][1], none_sums], axis=1),
                jnp.concatenate([none_sums, terms[1][1]], axis=1),
            ],
            axis=0,
        )
        lhs = jnp.concatenate([lhs_ref[tiles[0]], lhs_ref[tiles[1]]], axis=1)
        shared = pull_sums(lhs, rhs, sums)
        for side, tile in enumerate(tiles):
            acc = accs[side] + shared[16 * side : 16 * side + 16]
            out_ref[:, pl.ds(pl.multiple_of(tile * TILE, TILE), TILE)] = acc[0:8] + acc[8:16]
        return carry

    lax.fori_loop(0, lhs_ref.shape[0] // 2, two_tiles, 0, unroll=UNROLL // 2)


def other_layer_kernel(
    names_ref, flags_ref, layer_ref, lhs_ref, below_ref, own_ref, above_ref,
    sums_ref, vel_ref, body_ref, react_ref, disp_out_ref, vel_out_ref, table_ref,
):
    layer = layer_ref[0]
    for side, ref, edge in ((0, below_ref, 0), (1, above_ref, 3)):

        @pl.when(layer == edge)
        def _():
            for sector in range(5):
                fill_table(own_ref, table_ref, sector * 8, sector * 2 + side, 512)

        @pl.when(layer != edge)
        def _():
            for sector in range(5):
                fill_table(ref, table_ref, sector * 8, sector * 2 + side, 512)

    def one_tile(tile, carry):
        lanes = pl.ds(pl.multiple_of(tile * TILE, TILE), TILE)
        word = flags_ref[tile // 2]
        acc = pair_sums(tile, other_slots, table_ref, names_ref, word, lhs_ref[tile])
        acc = acc[0:8] + acc[8:16] + sums_ref[:, lanes]
        own = own_ref[16:24, lanes]
        disp = own[3:6]
        now = own[0:3] + disp
        whole = 1.0 - own[6:7]
        inner = acc[0:3] - now * acc[6:7]
        outer = acc[3:6] - now * acc[7:8]
        force = force_scale * whole * (own[7:8] * inner + outer)
        force += react_ref[:, lanes]
        for c in range(3):
            load = force[c : c + 1] + body_ref[c, :, lanes]
            vel = vel_ref[c, :, lanes] + time_step * load
            vel_out_ref[c, :, lanes] = vel
            disp_out_ref[c, :, lanes] = disp[c : c + 1] + time_step * vel
        return carry

    lax.fori_loop(0, lhs_ref.shape[0], one_tile, 0, unroll=UNROLL_OTHER)


def cost(flops):
    return pl.CostEstimate(flops=flops, transcendentals=0, bytes_accessed=6_000_000)


smem = pl.BlockSpec(memory_space=pltpu.SMEM)
vmem = pl.BlockSpec(memory_space=pltpu.VMEM)


def own_layer_sums(names, flags, lhs, blocks):
    points = blocks[0].shape[1]
    return pl.pallas_call(
        own_layer_kernel,
        out_shape=jax.ShapeDtypeStruct((8, points), f32),
        in_specs=[smem, smem] + [vmem] * (1 + len(blocks)),
        out_specs=vmem,
        scratch_shapes=[pltpu.VMEM((len(blocks), 48, points), bf16)],
        name="own_layer",
        cost_estimate=cost(18_000_000_000),
    )(names, flags, lhs, *blocks)


def other_layer_update(names, flags, layer, lhs, below, own, above, sums, vel, body, react):
    points = own.shape[1]
    shape = jax.ShapeDtypeStruct((3, 1, points), f32)
    return pl.pallas_call(
        other_layer_kernel,
        out_shape=(shape, shape),
        in_specs=[smem] * 3 + [vmem] * 8,
        out_specs=(vmem, vmem),
        scratch_shapes=[pltpu.VMEM((10, 48, points), bf16)],
        name="other_layer",
        cost_estimate=cost(36_000_000_000),
    )(names, flags, layer, lhs, below, own, above, sums, vel, body, react)


def parts32(value):
    high, middle, low = split3(value)
    return jnp.concatenate([high, middle, low, jnp.zeros_like(low)], axis=0)


def parts16(value):
    row = lax.broadcasted_iota(jnp.int32, value.shape, 0)
    high, middle, low = split3(value)
    return jnp.concatenate([jnp.where(row < 3, pltpu.roll(middle, 5, 0), high), low], axis=0)


def join16(value):
    return value[3:6] + value[0:3] + value[11:14]


def join32(value):
    return value[0:8] + value[8:16] + value[16:24]


def one_hot(index, count):
    row = lax.broadcasted_iota(jnp.int32, (count, index.shape[1]), 0)
    return jnp.where(row == index, 1.0, 0.0).astype(bf16)


def slot_row(index_ref):
    return jnp.concatenate([index_ref[c : c + 1, :] for c in range(index_ref.shape[0])], axis=1)


def values_kernel(
    pos_ref, disp_ref, damage_ref, modulus_ref, blade_ref, rim_ref, root_ref, field_ref, out_ref, pad_ref
):
    for c in range(3):
        field_ref[c : c + 1, :] = pos_ref[c]
        field_ref[3 + c : 4 + c, :] = disp_ref[c]
    field_ref[6:7, :] = damage_ref[...]
    field_ref[7:8, :] = modulus_ref[...]
    rim = slot_row(rim_ref)
    root = slot_row(root_ref)
    tile_of = lax.shift_right_logical(rim, 7)
    lane_hot = one_hot(rim & 127, TILE)

    def one_batch(step, acc):
        rows = []
        for inner in range(8):
            start = pl.multiple_of(step * (8 * TILE) + inner * TILE, TILE)
            rows.append(parts16(field_ref[:, pl.ds(start, TILE)]))
        found = jnp.dot(jnp.concatenate(rows, axis=0).astype(bf16), lane_hot, preferred_element_type=f32)
        for inner in range(8):
            acc = acc + jnp.where(tile_of == step * 8 + inner, found[inner * 16 : inner * 16 + 16], 0.0)
        return acc

    acc = lax.fori_loop(0, field_ref.shape[1] // (8 * TILE), one_batch, jnp.zeros((16, rim.shape[1]), f32))
    at_rim = join16(acc)
    pad_ref[...] = jnp.zeros_like(pad_ref)
    for c in range(3):
        pad_ref[c : c + 1] = blade_ref[c]
    found = jnp.dot(
        parts32(pad_ref[...]).astype(bf16), one_hot(root, blade_ref.shape[2]), preferred_element_type=f32
    )
    values = jnp.concatenate([at_rim, join32(found)[0:3]], axis=0)
    width = rim_ref.shape[1]
    for c in range(rim_ref.shape[0]):
        out_ref[:, c, :] = values[:, c * width : (c + 1) * width]


def coupling_values(pos, disp, damage, modulus, blade, rim, root):
    return pl.pallas_call(
        values_kernel,
        out_shape=(
            jax.ShapeDtypeStruct((8, pos.shape[2]), f32),
            jax.ShapeDtypeStruct((6, *rim.shape), f32),
        ),
        scratch_shapes=[pltpu.VMEM((8, blade.shape[2]), f32)],
        name="coupling_values",
        cost_estimate=cost(3_000_000_000),
    )(pos, disp, damage, modulus, blade, rim, root)


def slot_values(values_ref):
    return jnp.concatenate([values_ref[:, c, :] for c in range(values_ref.shape[1])], axis=1)


def coupling_kernel(
    swapped_ref, sent_ref, rim_ref, root_ref, nodes_ref, scale_ref, stiff_ref, blade_ref, vel_ref,
    after_ref, react_ref, disp_out_ref, vel_out_ref, pad_ref, elem_ref,
):
    nodes = blade_ref.shape[2]
    rim = slot_row(rim_ref)
    root = slot_row(root_ref)
    tile_of = lax.shift_right_logical(rim, 7)
    lane_hot = one_hot(rim & 127, TILE)
    pad_ref[...] = jnp.zeros_like(pad_ref)
    swapped = slot_values(swapped_ref)
    sent = slot_values(sent_ref)
    pad_ref[3:6] = spring * (swapped[3:6] - sent[0:3])
    back = parts16(pad_ref[...])
    pad_ref[...] = jnp.zeros_like(pad_ref)

    def one_batch(step, carry):
        rows = jnp.concatenate(
            [jnp.where(tile_of == step * 8 + inner, back, 0.0) for inner in range(8)], axis=0
        )
        put = lax.dot_general(rows.astype(bf16), lane_hot, across, preferred_element_type=f32)
        for inner in range(8):
            start = pl.multiple_of(step * (8 * TILE) + inner * TILE, TILE)
            react_ref[:, pl.ds(start, TILE)] = join16(put[inner * 16 : inner * 16 + 16])
        return carry

    lax.fori_loop(0, react_ref.shape[1] // (8 * TILE), one_batch, 0)
    pad_ref[0:3] = spring * (swapped[0:3] - sent[3:6])
    loads = parts32(pad_ref[...]).astype(bf16)
    coupling = join32(
        lax.dot_general(loads, one_hot(root, nodes), across, preferred_element_type=f32)
    )
    for c in range(3):
        pad_ref[c : c + 1] = blade_ref[c]
    blade = parts32(pad_ref[...]).astype(bf16)
    hots = []
    for q in range(8):
        hot = one_hot(nodes_ref[q : q + 1], nodes)
        hots.append(hot)
        taken = join32(jnp.dot(blade, hot, preferred_element_type=f32))
        for a in range(3):
            elem_ref[8 * a + q : 8 * a + q + 1, :] = taken[a : a + 1]
    force = scale_ref[...] * jnp.dot(
        stiff_ref[...], elem_ref[...], precision=lax.Precision.HIGHEST, preferred_element_type=f32
    )
    high, middle, low = split3(force)
    force = jnp.concatenate([high, middle, low, jnp.zeros((8, force.shape[1]), f32)], axis=0).astype(bf16)
    row = lax.broadcasted_iota(jnp.int32, (24, nodes), 0)
    total = jnp.zeros((24, nodes), f32)
    for q in range(8):
        put = lax.dot_general(force, hots[q], across, preferred_element_type=f32)
        total = total + jnp.where(row % 8 == q, put[0:24] + put[24:48] + put[48:72], 0.0)
    for a in range(3):
        internal = -jnp.sum(total[8 * a : 8 * a + 8], axis=0, keepdims=True)
        vel = vel_ref[a] + time_step * (internal + coupling[a : a + 1])
        vel_out_ref[a] = vel
        disp_out_ref[a] = blade_ref[a] + time_step * vel


def coupling_update(swapped, sent, rim, root, nodes, scale, stiff, blade, vel, after, points):
    small = jax.ShapeDtypeStruct(blade.shape, f32)
    return pl.pallas_call(
        coupling_kernel,
        out_shape=(jax.ShapeDtypeStruct((3, points), f32), small, small),
        scratch_shapes=[
            pltpu.VMEM((8, blade.shape[2]), f32),
            pltpu.VMEM((24, nodes.shape[1]), f32),
        ],
        in_specs=[vmem] * 9 + [pl.BlockSpec(memory_space=pl.ANY)],
        name="coupling_update",
        cost_estimate=cost(4_000_000_000),
    )(swapped, sent, rim, root, nodes, scale, stiff, blade, vel, after)


def stack_kernel(*refs):
    for place, ref in enumerate(refs[:-1]):
        refs[-1][8 * place : 8 * place + 8, :] = ref[...]


def stacked(blocks):
    return pl.pallas_call(
        stack_kernel,
        out_shape=jax.ShapeDtypeStruct((8 * len(blocks), blocks[0].shape[1]), f32),
        name="stacked",
    )(*blocks)


def shift_layer(value, by):
    size = lax.axis_size("layer")
    pairs = [(i, i + by) for i in range(size) if 0 <= i + by < size]
    return lax.ppermute(value, "layer", pairs)


def shift_sector(value, by):
    size = lax.axis_size("blk")
    return lax.ppermute(value, "blk", [(i, (i + by) % size) for i in range(size)])


def on_device(
    ref_pos,
    disk_disp,
    disk_vel,
    damage,
    modulus,
    body_load,
    nbr_tiles,
    break_flags,
    blade_disp,
    blade_vel,
    elem_nodes,
    elem_modulus,
    elem_stiff,
    root_nodes,
    rim_points,
):
    names = nbr_tiles[0, 0].T
    flags = break_flags[0, 0]
    rim = rim_points[0, 0].T
    root = root_nodes[0, 0].T
    blade_rows = blade_disp.reshape(3, 1, -1)
    field, sent = coupling_values(
        ref_pos.reshape(3, 1, -1), disk_disp.reshape(3, 1, -1), damage[0], modulus[0], blade_rows, rim, root
    )
    ahead = shift_sector(field, -1)
    far_ahead = shift_sector(field, -2)
    far_behind = shift_sector(field, 2)
    behind = shift_sector(field, 1)
    swapped = lax.all_to_all(sent, "blk", split_axis=2, concat_axis=2, tiled=True)
    lhs = own_table(field)
    blocks = [far_behind, behind, field, ahead, far_ahead]
    own = stacked(blocks)
    below = shift_layer(own, 1)
    above = shift_layer(own, -1)
    sums = own_layer_sums(names, flags, lhs, blocks)
    swapped, sums = lax.optimization_barrier((swapped, sums))
    reaction, blade_disp_new, blade_vel_new = coupling_update(
        swapped, sent, rim, root, elem_nodes[0, 0], elem_modulus[0], elem_stiff, blade_rows,
        blade_vel.reshape(3, 1, -1), sums, field.shape[1],
    )
    layer = lax.axis_index("layer").reshape(1).astype(jnp.int32)
    disk_disp_new, disk_vel_new = other_layer_update(
        names, flags, layer, lhs, below, own, above, sums, disk_vel.reshape(3, 1, -1),
        body_load.reshape(3, 1, -1), reaction
    )
    return (
        disk_disp_new.reshape(disk_disp.shape),
        disk_vel_new.reshape(disk_vel.shape),
        blade_disp_new.reshape(blade_disp.shape),
        blade_vel_new.reshape(blade_vel.shape),
    )


def solution(mesh):
    in_specs = (
        P("blk", "layer", None, None),
        P("blk", "layer", None, None),
        P("blk", "layer", None, None),
        P("blk", "layer", None),
        P("blk", "layer", None),
        P("blk", "layer", None, None),
        P("blk", "layer", None, None),
        P("blk", "layer", None),
        P("blk", "layer", None, None),
        P("blk", "layer", None, None),
        P("blk", "layer", None, None),
        P("blk", "layer", None),
        P(),
        P("blk", "layer", None, None),
        P("blk", "layer", None, None),
    )
    out_specs = (
        P("blk", "layer", None, None),
        P("blk", "layer", None, None),
        P("blk", "layer", None, None),
        P("blk", "layer", None, None),
    )
    return jax.shard_map(
        on_device, mesh=mesh, in_specs=in_specs, out_specs=out_specs, check_vma=False
    )
```
